1024 devices in a mesh: feat: 128 (over x_hi, z, core), row: 4 (over y), rep: 2 (over x_lo).
Axes of the slice: x: 4 (x_hi: 2, x_lo: 2; x = x_hi * 2 + x_lo), y: 4, z: 32, core: 2. Of those that a mesh axis runs over, the one named last changes fastest.
Arguments:
- activations: bfloat16 [512, 4608], P('feat', ('row', 'rep')), may hold values from -6 to 6
- enc_weight: bfloat16 [4608, 65536], P(('row', 'rep'), 'feat'), may hold values from -0.09375 to 0.09375
- enc_bias: float32 [65536], P('feat'), may hold values from -3 to 3
- dec_weight: bfloat16 [65536, 4608], P('feat', ('row', 'rep')), may hold values from -0.0234375 to 0.0234375
- dec_bias: float32 [4608], P(('row', 'rep')), may hold values from -3 to 3
- first_moment: bfloat16 [65536, 4608], P('feat', ('row', 'rep')), may hold values from -0.059814453 to 0.059814453
- second_moment: bfloat16 [65536, 4608], P('feat', ('row', 'rep')), may hold values from 9.953976e-06 to 0.0009994507
Outputs:
- reconstruction: bfloat16 [512, 4608], P('feat', ('row', 'rep'))
- dec_step: bfloat16 [65536, 4608], P('feat', ('row', 'rep'))
The draws below stay inside these ranges and needn't reach their ends.
All inputs are finite; a program needn't handle non-finite values.
Results may differ from the reference program's by a relative error of at most 0.0053.
Values may be sent and summed in bfloat16 or wider, within the bound.
A program may use at most 32 MiB of HBM per device.

```python
import math
import jax
import jax.numpy as jnp
from jax import lax

D = 4608
F = 65536
ROWS = 512


def level_of(stream_key, shape, pieces, low, high):
    factor_of, own = 1.0, jax.random.fold_in(stream_key, 6)
    for dim, parts in pieces:
        steps = jnp.exp(jax.random.uniform(jax.random.fold_in(own, dim), (parts,), jnp.float32, low / len(pieces), high / len(pieces)))
        factor_of = factor_of * jnp.repeat(steps, shape[dim] // parts).reshape([-1 if axis == dim else 1 for axis in range(len(shape))])
    return factor_of


def centred(stream_key, dims, spread, bound, cuts=(), dtype=jnp.bfloat16):
    values = jax.random.normal(stream_key, dims, jnp.float32) * spread
    if len(cuts) > 0:
        values = level_of(stream_key, dims, cuts, -0.22, 0.18) * values
    return jnp.clip(values, min=-bound, max=bound).astype(dtype)


def setup_inputs(seed: int = 0) -> dict:
    arg_keys = jax.random.split(jax.random.key(seed), 8)
    return {
        "activations": centred(arg_keys[0], (ROWS, D), 1.0, 6.0, ((0, 128), (1, 8))),
        "enc_weight": centred(arg_keys[1], (D, F), D ** -0.5, 0.09375, ((0, 8), (1, 128))),
        "enc_bias": centred(arg_keys[2], (F,), 0.5, 3.0, ((0, 128),), jnp.float32),
        "dec_weight": centred(arg_keys[3], (F, D), F ** -0.5, 0.0234375, ((0, 128), (1, 8))),
        "dec_bias": centred(arg_keys[4], (D,), 0.5, 3.0, ((0, 8),), jnp.float32),
        "first_moment": centred(arg_keys[5], (F, D), 0.01, 0.059814453, ((0, 128), (1, 8))),
        "second_moment": jnp.clip(jnp.exp(math.log(0.0009994507) - 4.609234 * jax.random.uniform(arg_keys[6], (F, D), jnp.float32) ** level_of(arg_keys[6], (F, D), ((0, 128), (1, 8)), -0.2, 0.2)), 9.953975677490234e-06, 0.0009994507).astype(jnp.bfloat16),
    }


sparsity_coef = 5.0
beta_one = 0.9
beta_two = 0.999
bias_one = 0.99997344
bias_two = 0.095207853
adam_eps = 1e-08
norm_eps = 1e-06

def adam_block(weight, first, second, active_block, count_block, residual):
    wide = weight.astype(jnp.float32)
    row_norm = jnp.sqrt(lax.optimization_barrier(jnp.sum(wide * wide, axis=1)) + norm_eps)
    product = lax.dot_general(active_block, residual, (((0,), (0,)), ((), ())), preferred_element_type=jnp.float32)
    gradient = 2.0 / ROWS * product + sparsity_coef / ROWS * count_block[:, None] * wide / row_norm[:, None]
    moment_one = beta_one * first.astype(jnp.float32) + (1.0 - beta_one) * gradient
    moment_two = beta_two * second.astype(jnp.float32) + (1.0 - beta_two) * gradient * gradient
    return (moment_one / bias_one / (jnp.sqrt(moment_two / bias_two) + adam_eps)).astype(jnp.bfloat16)

def reference(activations, enc_weight, enc_bias, dec_weight, dec_bias, first_moment, second_moment):
    centered = (activations.astype(jnp.float32) - dec_bias).astype(jnp.bfloat16)
    pre_sum = jnp.dot(centered, enc_weight, preferred_element_type=jnp.float32) + enc_bias
    active = jnp.maximum(pre_sum, 0.0).astype(jnp.bfloat16)
    rebuilt = jnp.dot(active, dec_weight, preferred_element_type=jnp.float32) + dec_bias
    residual = (rebuilt - activations.astype(jnp.float32)).astype(jnp.bfloat16)
    counts = lax.optimization_barrier(jnp.sum(active.astype(jnp.float32), axis=0))
    block = math.gcd(F, 4096)
    blocks = F // block
    active_split = active.reshape(ROWS, blocks, block).transpose(1, 0, 2)

    def one_block(items):
        return adam_block(items[0], items[1], items[2], items[3], items[4], residual)
    dec_step = lax.map(one_block, (dec_weight.reshape(blocks, block, D), first_moment.reshape(blocks, block, D), second_moment.reshape(blocks, block, D), active_split, counts.reshape(blocks, block)))
    return (rebuilt.astype(jnp.bfloat16), dec_step.reshape(F, D))
```

```python
import jax
import jax.numpy as jnp
from jax import lax
from jax.experimental import pallas as pl
from jax.experimental.pallas import tpu as pltpu
from jax.sharding import PartitionSpec as P

sparsity_coef = 5.0
beta_one = 0.9
beta_two = 0.999
bias_one = 0.99997344
bias_two = 0.095207853
adam_eps = 1e-08
norm_eps = 1e-06

MESH = pl.DeviceIdType.MESH
F32 = jnp.float32
BF16 = jnp.bfloat16


def make_kernel(nz, rows, reps, local_rows, width, feats):
    half = nz // 2
    peers = rows * reps
    chip_rows = 2 * local_rows
    total_rows = 2 * nz * chip_rows
    group = total_rows // peers
    per_far = peers // 2
    blocks = group // chip_rows
    core_groups = per_far // 2

    def kernel(
        act_ref, enc_hbm, ebias_ref, dec_hbm, dbias_ref, first_hbm, second_hbm,
        recon_ref, step_hbm,
        enc, dec, first, second, step, load_sem, store_sem,
        act_send, act_recv, acts, gathered, block, partial, sums_out, sums_in, active, active_t,
        squares_out, squares_in, product, core_in, x_out, x_in, z_out, z_in, total_out, total_in, residuals, coef,
        pair_send, pair_recv, z_send, z_recv, zr_send, zr_recv, za_send, za_recv,
        peer_send, peer_recv, sq_send, sq_recv, ac_send, ac_recv,
    ):
        feat = lax.axis_index("feat")
        row, rep = lax.axis_index("row"), lax.axis_index("rep")
        far_x = lax.div(feat, 2 * nz)
        z = lax.rem(lax.div(feat, 2), nz)
        core = lax.rem(feat, 2)
        k = row * reps + rep

        def at_z(where):
            return (far_x * (2 * nz) + lax.rem(where + 2 * nz, nz) * 2 + core, row, rep)

        other_core = (feat + 1 - 2 * core, row, rep)
        other_x = (lax.rem(feat + 2 * nz, 4 * nz), row, rep)

        def peer(j):
            p = lax.rem(k + j, peers)
            return (feat, lax.div(p, reps), lax.rem(p, reps))

        loads = [
            pltpu.make_async_copy(src, dst, load_sem.at[i])
            for i, (src, dst) in enumerate(
                ((dec_hbm, dec), (enc_hbm, enc), (first_hbm, first), (second_hbm, second))
            )
        ]
        for load in loads:
            load.start()

        barrier = pltpu.get_barrier_semaphore()

        def greet(device):
            pl.semaphore_signal(barrier, inc=1, device_id=device, device_id_type=MESH)

        low = core * half

        @pl.loop(0, half)
        def _(i):
            s = low + i

            @pl.when(s > 0)
            def _():
                greet(at_z(z + s))
                greet(at_z(z - s))

        greet(other_core)
        greet(other_x)

        @pl.loop(1, peers)
        def _(j):
            greet(peer(j))

        act_send[...] = act_ref[...]
        loads[0].wait()
        wide = dec[...].astype(F32)
        square = wide * wide
        high = square.astype(BF16)
        rest = (square - high.astype(F32)).astype(BF16)
        ones = jnp.ones((8, width), BF16)
        along = (((1,), (1,)), ((), ()))
        squares_out[...] = lax.dot_general(ones, high, along, preferred_element_type=F32) + lax.dot_general(
            ones, rest, along, preferred_element_type=F32
        )
        pl.semaphore_wait(barrier, 2 * half - 2 * (1 - core) + 2 + peers - 1)

        def pair(src, dst, i, device):
            return pltpu.make_async_remote_copy(
                src_ref=src, dst_ref=dst, send_sem=pair_send.at[i], recv_sem=pair_recv.at[i],
                device_id=device, device_id_type=MESH,
            )

        def square_copy(j):
            return pltpu.make_async_remote_copy(
                src_ref=squares_out, dst_ref=squares_in.at[j], send_sem=sq_send.at[j], recv_sem=sq_recv.at[j],
                device_id=peer(j), device_id_type=MESH,
            )

        swap = pair(act_send, act_recv, 0, other_core)
        swap.start()
        swap.wait()
        own, his = act_send[...].astype(F32), act_recv[...].astype(F32)
        acts[0:local_rows] = jnp.where(core == 0, own, his)
        acts[local_rows:] = jnp.where(core == 0, his, own)
        block[...] = (acts[...] - dbias_ref[...]).astype(BF16)

        def gather(src, buffer, send, recv, first_pair, between):
            def z_copy(i):
                s = jnp.where(core == 0, half - 1 - i, half + i)
                return s, pltpu.make_async_remote_copy(
                    src_ref=src, dst_ref=buffer.at[0, s], send_sem=send.at[i], recv_sem=recv.at[i],
                    device_id=at_z(z + s), device_id_type=MESH,
                )

            @pl.loop(0, half)
            def _(i):
                s, copy = z_copy(i)

                @pl.when(s > 0)
                def _():
                    copy.start()

            @pl.when(core == 0)
            def _():
                buffer[0, 0] = src[...]

            between()

            @pl.loop(0, half)
            def _(i):
                s, copy = z_copy(i)

                @pl.when(s > 0)
                def _():
                    copy.wait_recv()

            mine = pl.ds(low, half)
            to_x = pair(buffer.at[0, mine], buffer.at[1, mine], first_pair, other_x)
            to_core = pair(buffer.at[0, mine], buffer.at[0, mine], first_pair + 1, other_core)
            on_core = pair(buffer.at[1, mine], buffer.at[1, mine], first_pair + 2, other_core)
            to_x.start()
            to_core.start()
            return to_x, to_core, on_core, z_copy

        def finish_sends(z_copy):
            @pl.loop(0, half)
            def _(i):
                s, copy = z_copy(i)

                @pl.when(s > 0)
                def _():
                    copy.wait_send()

        def during_first():
            @pl.loop(1, peers)
            def _(j):
                square_copy(j).start()

            loads[1].wait()

        to_x, to_core, on_core, z_copy_a = gather(block, gathered, z_send, z_recv, 1, during_first)

        def sum_copy(j):
            p = lax.rem(k + j, peers)
            return p, pltpu.make_async_remote_copy(
                src_ref=sums_out.at[p], dst_ref=sums_in.at[j], send_sem=peer_send.at[j], recv_sem=peer_recv.at[j],
                device_id=peer(j), device_id_type=MESH,
            )

        def encode(far):
            rows_in = gathered[far].reshape(nz * chip_rows, width)
            value = jnp.dot(rows_in, enc[...], preferred_element_type=F32).reshape(per_far, group, feats)
            partial[far * per_far : (far + 1) * per_far] = value
            sums_out[far * per_far : (far + 1) * per_far] = value.astype(BF16)

            @pl.loop(1, peers)
            def _(j):
                p, copy = sum_copy(j)

                @pl.when(lax.div(p, per_far) == far)
                def _():
                    copy.start()

        to_core.wait_recv()
        encode(0)
        to_x.wait_recv()
        on_core.start()
        on_core.wait_recv()
        encode(1)

        pre_sum = partial[k] + ebias_ref[...]
        for j in range(1, peers):
            sum_copy(j)[1].wait_recv()
            pre_sum += sums_in[j].astype(F32)
        active[k] = jnp.maximum(pre_sum, 0.0).astype(BF16)

        def active_copy(j):
            return pltpu.make_async_remote_copy(
                src_ref=active.at[k], dst_ref=active.at[k], send_sem=ac_send.at[j], recv_sem=ac_recv.at[j],
                device_id=peer(j), device_id_type=MESH,
            )

        @pl.loop(1, peers)
        def _(j):
            active_copy(j).start()

        @pl.loop(1, peers)
        def _(j):
            active_copy(j).wait_recv()

        his_low = half - low

        def decode(far, who):
            rows_in = active[pl.ds(far * per_far + who * core_groups, core_groups)]
            value = jnp.dot(
                rows_in.reshape(half * chip_rows, feats), dec[...], preferred_element_type=F32
            )
            product[far, pl.ds(who * half, half)] = value.reshape(half, chip_rows, width)

        core_copies = [
            pair(product.at[far, pl.ds(his_low, half)], core_in.at[far], 4 + far, other_core) for far in (0, 1)
        ]
        decode(1, 1 - core)
        core_copies[1].start()
        decode(0, 1 - core)
        core_copies[0].start()
        decode(1, core)
        core_copies[1].wait_recv()
        x_out[...] = (product[1, pl.ds(low, half)] + core_in[1]).astype(BF16)
        over = pair(x_out, x_in, 6, other_x)
        over.start()
        decode(0, core)
        core_copies[0].wait_recv()
        near = product[0, pl.ds(low, half)] + core_in[0]
        over.wait_recv()
        z_out[...] = (near + x_in[...].astype(F32)).astype(BF16)

        def back_copy(i):
            place = jnp.where(core == 0, half - 1 - i, i)
            s = low + place
            return s, pltpu.make_async_remote_copy(
                src_ref=z_out.at[place], dst_ref=z_in.at[place], send_sem=zr_send.at[i], recv_sem=zr_recv.at[i],
                device_id=at_z(z - s), device_id_type=MESH,
            )

        @pl.loop(0, half)
        def _(i):
            s, copy = back_copy(i)

            @pl.when(s > 0)
            def _():
                copy.start()

        @pl.when(core == 0)
        def _():
            z_in[0] = z_out[0]

        flat = active[...].reshape(total_rows, feats)
        active_t[...] = flat.T
        counts = jnp.dot(active_t[...], jnp.ones((total_rows, 128), BF16), preferred_element_type=F32)
        sum_squares = squares_out[...]
        for j in range(1, peers):
            square_copy(j).wait_recv()
            sum_squares += squares_in[j]
        norm = jnp.sqrt(sum_squares[0:1] + norm_eps)
        norm = jnp.broadcast_to(norm, (128, feats)).T
        coef[...] = sparsity_coef / total_rows * counts / norm

        @pl.loop(0, half)
        def _(i):
            s, copy = back_copy(i)

            @pl.when(s > 0)
            def _():
                copy.wait_recv()

        total_out[...] = jnp.sum(z_in[...].astype(F32), axis=0)
        both = pair(total_out, total_in, 7, other_core)
        both.start()
        both.wait_recv()
        rebuilt = total_out[...] + total_in[...] + dbias_ref[...]
        recon_ref[...] = jnp.where(core == 0, rebuilt[0:local_rows], rebuilt[local_rows:]).astype(BF16)
        block_two = z_out.at[0]
        finish_sends(back_copy)
        block_two[...] = (rebuilt - acts[...]).astype(BF16)

        def during_last():
            loads[2].wait()
            loads[3].wait()

        to_x_two, to_core_two, on_core_two, z_copy_b = gather(
            block_two, residuals, za_send, za_recv, 8, during_last
        )
        to_core_two.wait_recv()
        to_x_two.wait_recv()
        on_core_two.start()
        on_core_two.wait_recv()
        all_residual = residuals[...].reshape(total_rows, width)

        part = feats // 4

        def store(i):
            where = pl.ds(i * part, part)
            return pltpu.make_async_copy(step.at[where], step_hbm.at[where], store_sem.at[i])

        for i in range(4):
            where = slice(i * part, (i + 1) * part)
            gradient = 2.0 / total_rows * jnp.dot(
                active_t[where], all_residual, preferred_element_type=F32
            ) + coef[where, 0:1] * dec[where].astype(F32)
            moment_one = beta_one * first[where].astype(F32) + (1.0 - beta_one) * gradient
            moment_two = beta_two * second[where].astype(F32) + (1.0 - beta_two) * gradient * gradient
            step[where] = (
                moment_one * (1.0 / bias_one) / (jnp.sqrt(moment_two * (1.0 / bias_two)) + adam_eps)
            ).astype(BF16)
            store(i).start()

        finish_sends(z_copy_a)
        finish_sends(z_copy_b)
        for copy in (to_x, to_core, on_core, *core_copies, over, both, to_x_two, to_core_two, on_core_two):
            copy.wait_send()

        @pl.loop(1, peers)
        def _(j):
            square_copy(j).wait_send()
            sum_copy(j)[1].wait_send()
            active_copy(j).wait_send()

        for i in range(4):
            store(i).wait()

    scratch = [
        pltpu.VMEM((width, feats), BF16),
        pltpu.VMEM((feats, width), BF16),
        pltpu.VMEM((feats, width), BF16),
        pltpu.VMEM((feats, width), BF16),
        pltpu.VMEM((feats, width), BF16),
        pltpu.SemaphoreType.DMA((4,)),
        pltpu.SemaphoreType.DMA((4,)),
        pltpu.VMEM((local_rows, width), BF16),
        pltpu.VMEM((local_rows, width), BF16),
        pltpu.VMEM((chip_rows, width), F32),
        pltpu.VMEM((2, nz, chip_rows, width), BF16),
        pltpu.VMEM((chip_rows, width), BF16),
        pltpu.VMEM((peers, group, feats), F32),
        pltpu.VMEM((peers, group, feats), BF16),
        pltpu.VMEM((peers, group, feats), BF16),
        pltpu.VMEM((peers, group, feats), BF16),
        pltpu.VMEM((feats, total_rows), BF16),
        pltpu.VMEM((8, feats), F32),
        pltpu.VMEM((peers, 8, feats), F32),
        pltpu.VMEM((2, nz, chip_rows, width), F32),
        pltpu.VMEM((2, half, chip_rows, width), F32),
        pltpu.VMEM((half, chip_rows, width), BF16),
        pltpu.VMEM((half, chip_rows, width), BF16),
        pltpu.VMEM((half, chip_rows, width), BF16),
        pltpu.VMEM((half, chip_rows, width), BF16),
        pltpu.VMEM((chip_rows, width), F32),
        pltpu.VMEM((chip_rows, width), F32),
        pltpu.VMEM((2, nz, chip_rows, width), BF16),
        pltpu.VMEM((feats, 128), F32),
        pltpu.SemaphoreType.DMA((11,)),
        pltpu.SemaphoreType.DMA((11,)),
        *(pltpu.SemaphoreType.DMA((half,)) for _ in range(6)),
        *(pltpu.SemaphoreType.DMA((peers,)) for _ in range(6)),
    ]
    return kernel, scratch


def shards(nz, rows, reps, activations, enc_weight, enc_bias, dec_weight, dec_bias, first_moment, second_moment):
    local_rows, width = activations.shape
    feats = enc_weight.shape[1]
    kernel, scratch = make_kernel(nz, rows, reps, local_rows, width, feats)
    vmem = pl.BlockSpec(memory_space=pltpu.VMEM)
    hbm = pl.BlockSpec(memory_space=pl.ANY)
    return pl.pallas_call(
        kernel,
        out_shape=(
            jax.ShapeDtypeStruct((local_rows, width), BF16),
            jax.ShapeDtypeStruct((feats, width), BF16),
        ),
        in_specs=[vmem, hbm, vmem, hbm, vmem, hbm, hbm],
        out_specs=(vmem, hbm),
        scratch_shapes=scratch,
        compiler_params=pltpu.CompilerParams(
            collective_id=0, has_side_effects=True, vmem_limit_bytes=48 * 2**20
        ),
    )(activations, enc_weight, enc_bias[None, :], dec_weight, dec_bias[None, :], first_moment, second_moment)


def solution(mesh):
    nz, rows, reps = mesh.shape["feat"] // 4, mesh.shape["row"], mesh.shape["rep"]

    def step(*args):
        return shards(nz, rows, reps, *args)

    return jax.shard_map(
        step,
        mesh=mesh,
        in_specs=(
            P("feat", ("row", "rep")),
            P(("row", "rep"), "feat"),
            P("feat"),
            P("feat", ("row", "rep")),
            P(("row", "rep")),
            P("feat", ("row", "rep")),
            P("feat", ("row", "rep")),
        ),
        out_specs=(P("feat", ("row", "rep")), P("feat", ("row", "rep"))),
        check_vma=False,
    )
```

```python
import jax
import jax.numpy as jnp
from jax import lax
from jax.experimental import pallas as pl
from jax.experimental.pallas import tpu as pltpu
from jax.sharding import PartitionSpec as P

sparsity_coef = 5.0
beta_one = 0.9
beta_two = 0.999
bias_one = 0.99997344
bias_two = 0.095207853
adam_eps = 1e-08
norm_eps = 1e-06

MESH = pl.DeviceIdType.MESH
F32 = jnp.float32
BF16 = jnp.bfloat16


def make_kernel(nz, rows, reps, local_rows, width, feats):
    near = (0, 1, 2, -1)
    window = len(near)
    per_chip = nz // window
    per_core = per_chip // 2
    chip_rows = 2 * local_rows
    total_rows = 2 * nz * chip_rows
    half_rows = total_rows // 2
    peers = rows * reps
    group = total_rows // peers
    core_rows = per_core * chip_rows
    assert peers == 2 * window and group == 2 * core_rows
    around = [(far, w) for far in (1, 0) for w in range(window) if (far, w) != (0, 0)]

    def kernel(
        act_ref, enc_hbm, ebias_ref, dec_hbm, dbias_ref, first_hbm, second_hbm,
        recon_ref, step_hbm,
        enc, dec, first, second, step, load_sem, store_sem,
        act_send, act_recv, acts, gathered, block, partial, sums_out, sums_in, active,
        squares_out, squares_in, product, core_in, parts_out, parts_in, z_out, z_in, total_out, total_in, residuals,
        block_two, coef, residual_t, slope,
        pair_send, pair_recv, z_send, z_recv, zr_send, zr_recv, za_send, za_recv,
        x_send, x_recv, c_send, c_recv, part_send, part_recv, xa_send, xa_recv, ca_send, ca_recv,
        peer_send, peer_recv, sq_send, sq_recv, ac_send, ac_recv,
    ):
        feat = lax.axis_index("feat")
        row, rep = lax.axis_index("row"), lax.axis_index("rep")
        far_x = lax.div(feat, 2 * nz)
        z = lax.rem(lax.div(feat, 2), nz)
        core = lax.rem(feat, 2)
        k = row * reps + rep

        def chip(far, where):
            x = lax.rem(far_x + far, 2)
            return (x * (2 * nz) + lax.rem(where + 2 * nz, nz) * 2 + core, row, rep)

        other_core = (feat + 1 - 2 * core, row, rep)

        def peer(j):
            p = lax.rem(k + j, peers)
            return (feat, lax.div(p, reps), lax.rem(p, reps))

        loads = [
            pltpu.make_async_copy(src, dst, load_sem.at[i])
            for i, (src, dst) in enumerate(
                ((dec_hbm, dec), (enc_hbm, enc), (first_hbm, first), (second_hbm, second))
            )
        ]
        for load in loads:
            load.start()

        barrier = pltpu.get_barrier_semaphore()

        def greet(device):
            pl.semaphore_signal(barrier, inc=1, device_id=device, device_id_type=MESH)

        def far_first(j):
            m = jnp.where(core == 0, j, per_chip - 1 - j)
            return m, m != per_core

        @pl.loop(0, per_core)
        def _(j):
            m, remote = far_first(j)

            @pl.when(remote)
            def _():
                greet(chip(0, z + window * (per_core - m)))
                greet(chip(0, z - window * (per_core - m)))

        beside = sorted({(far, side * near[w]) for far, w in around for side in (1, -1)})
        for far, offset in beside:
            greet(chip(far, z + offset))
        greet(other_core)

        @pl.loop(1, peers)
        def _(j):
            greet(peer(j))

        act_send[...] = act_ref[...]
        loads[0].wait()
        wide = dec[...].astype(F32)
        square = wide * wide
        high = square.astype(BF16)
        rest = (square - high.astype(F32)).astype(BF16)
        ones = jnp.ones((8, width), BF16)
        squares_out[...] = jnp.dot(ones, high, preferred_element_type=F32) + jnp.dot(
            ones, rest, preferred_element_type=F32
        )
        pl.semaphore_wait(barrier, 2 * per_core - 2 * core + len(beside) + peers)

        def pair(src, dst, i, device):
            return pltpu.make_async_remote_copy(
                src_ref=src, dst_ref=dst, send_sem=pair_send.at[i], recv_sem=pair_recv.at[i],
                device_id=device, device_id_type=MESH,
            )

        def square_copy(j):
            return pltpu.make_async_remote_copy(
                src_ref=squares_out, dst_ref=squares_in.at[j], send_sem=sq_send.at[j], recv_sem=sq_recv.at[j],
                device_id=peer(j), device_id_type=MESH,
            )

        swap = pair(act_send, act_recv, 0, other_core)
        swap.start()
        swap.wait()
        own, his = act_send[...].astype(F32), act_recv[...].astype(F32)
        acts[0:local_rows] = jnp.where(core == 0, own, his)
        acts[local_rows:] = jnp.where(core == 0, his, own)
        block[...] = (acts[...] - dbias_ref[...].reshape(1, width)).astype(BF16)

        def each_far(action):
            @pl.loop(0, per_core)
            def _(j):
                m, remote = far_first(j)

                @pl.when(remote)
                def _():
                    action(m)

        mine = pl.ds(core * per_core, per_core)

        def gather(src, buffer, z_sems, x_sems, core_sems, between):
            def z_copy(m):
                return pltpu.make_async_remote_copy(
                    src_ref=src, dst_ref=buffer.at[0, 0, m], send_sem=z_sems[0].at[m], recv_sem=z_sems[1].at[m],
                    device_id=chip(0, z + window * (per_core - m)), device_id_type=MESH,
                )

            def beside_copy(far, w):
                return pltpu.make_async_remote_copy(
                    src_ref=buffer.at[0, 0, mine], dst_ref=buffer.at[far, w, mine],
                    send_sem=x_sems[0].at[far * window + w], recv_sem=x_sems[1].at[far * window + w],
                    device_id=chip(far, z + near[w]), device_id_type=MESH,
                )

            def core_copy(far, w):
                return pltpu.make_async_remote_copy(
                    src_ref=buffer.at[far, w, mine], dst_ref=buffer.at[far, w, mine],
                    send_sem=core_sems[0].at[far * window + w], recv_sem=core_sems[1].at[far * window + w],
                    device_id=other_core, device_id_type=MESH,
                )

            each_far(lambda m: z_copy(m).start())

            @pl.when(core == 1)
            def _():
                buffer[0, 0, per_core] = src[...]

            between()
            each_far(lambda m: z_copy(m).wait_recv())
            for far, w in around:
                beside_copy(far, w).start()
            core_copy(0, 0).start()

            def arrive(far):
                for w in range(window):
                    if (far, w) != (0, 0):
                        beside_copy(far, w).wait_recv()
                        core_copy(far, w).start()
                for w in range(window):
                    core_copy(far, w).wait_recv()

            def finish():
                each_far(lambda m: z_copy(m).wait_send())
                for far, w in around:
                    beside_copy(far, w).wait_send()
                    core_copy(far, w).wait_send()
                core_copy(0, 0).wait_send()

            return arrive, finish

        def during_first():
            @pl.loop(1, peers)
            def _(j):
                square_copy(j).start()

            loads[1].wait()

        arrive, finish_first = gather(
            block, gathered, (z_send, z_recv), (x_send, x_recv), (c_send, c_recv), during_first
        )

        def sum_copy(j):
            p = lax.rem(k + j, peers)
            return p, pltpu.make_async_remote_copy(
                src_ref=sums_out.at[p], dst_ref=sums_in.at[j], send_sem=peer_send.at[j], recv_sem=peer_recv.at[j],
                device_id=peer(j), device_id_type=MESH,
            )

        def encode(far):
            rows_in = gathered[far].reshape(half_rows, width)
            value = jnp.dot(rows_in, enc[...], preferred_element_type=F32).reshape(window, group, feats)
            partial[far * window : (far + 1) * window] = value
            sums_out[far * window : (far + 1) * window] = value.astype(BF16)

            @pl.loop(1, peers)
            def _(j):
                p, copy = sum_copy(j)

                @pl.when(lax.div(p, window) == far)
                def _():
                    copy.start()

        arrive(0)
        encode(0)
        arrive(1)
        encode(1)

        pre_sum = partial[k] + ebias_ref[...].reshape(1, feats)
        for j in range(1, peers):
            sum_copy(j)[1].wait_recv()
            pre_sum += sums_in[j].astype(F32)
        active[k] = jnp.maximum(pre_sum, 0.0).reshape(2, core_rows, feats).astype(BF16)

        def active_copy(j):
            return pltpu.make_async_remote_copy(
                src_ref=active.at[k], dst_ref=active.at[k], send_sem=ac_send.at[j], recv_sem=ac_recv.at[j],
                device_id=peer(j), device_id_type=MESH,
            )

        @pl.loop(1, peers)
        def _(j):
            active_copy(j).start()

        def wait_active(far):
            @pl.loop(1, peers)
            def _(j):
                @pl.when(lax.div(lax.rem(k - j + peers, peers), window) == far)
                def _():
                    active_copy(j).wait_recv()

        def decode(far, who):
            value = lax.dot_general(
                active[far * window : (far + 1) * window, who].reshape(window * core_rows, feats),
                dec[...], (((1,), (1,)), ((), ())), preferred_element_type=F32,
            )
            product[far, who] = value.reshape(window, core_rows, width)

        core_parts = [pair(product.at[far, 1 - core], core_in.at[far], 1 + far, other_core) for far in (0, 1)]

        def part_copy(far, w):
            return pltpu.make_async_remote_copy(
                src_ref=parts_out.at[far, w], dst_ref=parts_in.at[far * window + w],
                send_sem=part_send.at[far * window + w], recv_sem=part_recv.at[far * window + w],
                device_id=chip(far, z - near[w]), device_id_type=MESH,
            )

        def hand_out(far):
            core_parts[far].wait_recv()
            both_cores = product[far, core] + core_in[far]
            parts_out[far] = both_cores.astype(BF16)
            for other, w in around:
                if other == far:
                    part_copy(far, w).start()
            return both_cores

        wait_active(0)
        decode(0, 1 - core)
        core_parts[0].start()
        decode(0, core)
        wait_active(1)
        decode(1, 1 - core)
        core_parts[1].start()
        own_part = hand_out(0)[0]
        decode(1, core)
        hand_out(1)
        for far, w in reversed(around):
            part_copy(far, w).wait_recv()
            own_part += parts_in[far * window + w].astype(F32)
        z_out[...] = own_part.reshape(per_core, chip_rows, width).astype(BF16)

        def back_copy(m):
            place = m - core * per_core
            return pltpu.make_async_remote_copy(
                src_ref=z_out.at[place], dst_ref=z_in.at[place], send_sem=zr_send.at[m], recv_sem=zr_recv.at[m],
                device_id=chip(0, z + window * (m - per_core)), device_id_type=MESH,
            )

        each_far(lambda m: back_copy(m).start())

        @pl.when(core == 1)
        def _():
            z_in[0] = z_out[0]

        flat = active[...].reshape(total_rows, feats)
        counts = jnp.dot(jnp.ones((8, total_rows), BF16), flat, preferred_element_type=F32)
        sum_squares = squares_out[...]
        for j in range(1, peers):
            square_copy(j).wait_recv()
            sum_squares += squares_in[j]
        norm = jnp.sqrt(sum_squares[0:1] + norm_eps)
        coef[...] = sparsity_coef / total_rows * counts[0:1] / norm

        each_far(lambda m: back_copy(m).wait_recv())
        total_out[...] = jnp.sum(z_in[...].astype(F32), axis=0)
        both = pair(total_out, total_in, 3, other_core)
        both.start()
        both.wait_recv()
        rebuilt = total_out[...] + total_in[...] + dbias_ref[...].reshape(1, width)
        recon_ref[...] = jnp.where(core == 0, rebuilt[0:local_rows], rebuilt[local_rows:]).astype(BF16)
        block_two[...] = (rebuilt - acts[...]).astype(BF16)

        def during_last():
            loads[2].wait()
            loads[3].wait()

        arrive, finish_last = gather(
            block_two, residuals, (za_send, za_recv), (xa_send, xa_recv), (ca_send, ca_recv), during_last
        )

        def turn(far):
            residual_t[:, far * half_rows : (far + 1) * half_rows] = residuals[far].reshape(half_rows, width).T

        arrive(0)
        turn(0)
        slope[...] = jnp.dot(
            residual_t[:, :half_rows], active[:window].reshape(half_rows, feats), preferred_element_type=F32
        )
        arrive(1)
        turn(1)

        part = width // 4

        def store(i):
            where = pl.ds(i * part, part)
            return pltpu.make_async_copy(step.at[where], step_hbm.at[where], store_sem.at[i])

        for i in range(4):
            where = slice(i * part, (i + 1) * part)
            slope_rest = jnp.dot(
                residual_t[where, half_rows:], active[window:].reshape(half_rows, feats),
                preferred_element_type=F32,
            )
            gradient = 2.0 / total_rows * (slope[where] + slope_rest) + coef[...] * dec[where].astype(F32)
            moment_one = beta_one * first[where].astype(F32) + (1.0 - beta_one) * gradient
            moment_two = beta_two * second[where].astype(F32) + (1.0 - beta_two) * gradient * gradient
            step[where] = (
                moment_one * (1.0 / bias_one) / (jnp.sqrt(moment_two * (1.0 / bias_two)) + adam_eps)
            ).astype(BF16)
            store(i).start()

        finish_first()
        finish_last()
        each_far(lambda m: back_copy(m).wait_send())
        for copy in (*core_parts, both):
            copy.wait_send()
        for far, w in around:
            part_copy(far, w).wait_send()

        @pl.loop(1, peers)
        def _(j):
            square_copy(j).wait_send()
            sum_copy(j)[1].wait_send()
            active_copy(j).wait_send()

        for i in range(4):
            store(i).wait()

    scratch = [
        *(pltpu.VMEM((width, feats), BF16) for _ in range(5)),
        pltpu.SemaphoreType.DMA((4,)),
        pltpu.SemaphoreType.DMA((4,)),
        pltpu.VMEM((local_rows, width), BF16),
        pltpu.VMEM((local_rows, width), BF16),
        pltpu.VMEM((chip_rows, width), F32),
        pltpu.VMEM((2, window, per_chip, chip_rows, width), BF16),
        pltpu.VMEM((chip_rows, width), BF16),
        pltpu.VMEM((peers, group, feats), F32),
        pltpu.VMEM((peers, group, feats), BF16),
        pltpu.VMEM((peers, group, feats), BF16),
        pltpu.VMEM((peers, 2, core_rows, feats), BF16),
        pltpu.VMEM((8, feats), F32),
        pltpu.VMEM((peers, 8, feats), F32),
        pltpu.VMEM((2, 2, window, core_rows, width), F32),
        pltpu.VMEM((2, window, core_rows, width), F32),
        pltpu.VMEM((2, window, core_rows, width), BF16),
        pltpu.VMEM((2 * window, core_rows, width), BF16),
        pltpu.VMEM((per_core, chip_rows, width), BF16),
        pltpu.VMEM((per_core, chip_rows, width), BF16),
        pltpu.VMEM((chip_rows, width), F32),
        pltpu.VMEM((chip_rows, width), F32),
        pltpu.VMEM((2, window, per_chip, chip_rows, width), BF16),
        pltpu.VMEM((chip_rows, width), BF16),
        pltpu.VMEM((1, feats), F32),
        pltpu.VMEM((width, total_rows), BF16),
        pltpu.VMEM((width, feats), F32),
        *(pltpu.SemaphoreType.DMA((4,)) for _ in range(2)),
        *(pltpu.SemaphoreType.DMA((per_chip,)) for _ in range(6)),
        *(pltpu.SemaphoreType.DMA((2 * window,)) for _ in range(10)),
        *(pltpu.SemaphoreType.DMA((peers,)) for _ in range(6)),
    ]
    return kernel, scratch


def shards(nz, rows, reps, activations, enc_weight, enc_bias, dec_weight, dec_bias, first_moment, second_moment):
    local_rows, width = activations.shape
    feats = enc_weight.shape[1]
    kernel, scratch = make_kernel(nz, rows, reps, local_rows, width, feats)
    vmem = pl.BlockSpec(memory_space=pltpu.VMEM)
    hbm = pl.BlockSpec(memory_space=pl.ANY)
    recon, step = pl.pallas_call(
        kernel,
        out_shape=(
            jax.ShapeDtypeStruct((local_rows, width), BF16),
            jax.ShapeDtypeStruct((width, feats), BF16),
        ),
        in_specs=[vmem, hbm, vmem, hbm, vmem, hbm, hbm],
        out_specs=(vmem, hbm),
        scratch_shapes=scratch,
        compiler_params=pltpu.CompilerParams(
            collective_id=0, has_side_effects=True, vmem_limit_bytes=60 * 2**20
        ),
    )(activations, enc_weight, enc_bias, dec_weight.T, dec_bias, first_moment.T, second_moment.T)
    return recon, step.T


def solution(mesh):
    nz, rows, reps = mesh.shape["feat"] // 4, mesh.shape["row"], mesh.shape["rep"]

    def step(*args):
        return shards(nz, rows, reps, *args)

    return jax.shard_map(
        step,
        mesh=mesh,
        in_specs=(
            P("feat", ("row", "rep")),
            P(("row", "rep"), "feat"),
            P("feat"),
            P("feat", ("row", "rep")),
            P(("row", "rep")),
            P("feat", ("row", "rep")),
            P("feat", ("row", "rep")),
        ),
        out_specs=(P("feat", ("row", "rep")), P("feat", ("row", "rep"))),
        check_vma=False,
    )
```

```python
import jax
import jax.numpy as jnp
from jax import lax
from jax.experimental import pallas as pl
from jax.experimental.pallas import tpu as pltpu
from jax.sharding import PartitionSpec as P

sparsity_coef = 5.0
beta_one = 0.9
beta_two = 0.999
bias_one = 0.99997344
bias_two = 0.095207853
adam_eps = 1e-08
norm_eps = 1e-06

MESH = pl.DeviceIdType.MESH
F32 = jnp.float32
BF16 = jnp.bfloat16


def make_kernel(nz, rows, reps, local_rows, width, feats):
    near = (0, 1, 2, -1)
    window = len(near)
    per_chip = nz // window
    per_core = per_chip // 2
    chip_rows = 2 * local_rows
    total_rows = 2 * nz * chip_rows
    half_rows = total_rows // 2
    peers = rows * reps
    group = total_rows // peers
    core_rows = per_core * chip_rows
    assert peers == 2 * window and group == 2 * core_rows
    around = [(far, w) for far in (1, 0) for w in range(window) if (far, w) != (0, 0)]

    def kernel(
        act_ref, enc_hbm, ebias_ref, dec_hbm, dbias_ref, first_hbm, second_hbm,
        recon_ref, step_hbm,
        enc, dec, first, second, step, load_sem, store_sem,
        act_send, act_recv, acts, gathered, block, partial, sums_out, sums_in, active,
        squares_out, squares_in, product, core_in, parts_out, parts_in, own_part, z_out, z_in, total_out, total_in, residuals,
        block_two, coef, residual_t, slope,
        pair_send, pair_recv, z_send, z_recv, zr_send, zr_recv, za_send, za_recv,
        x_send, x_recv, xa_send, xa_recv, c_send, c_recv, ca_send, ca_recv, part_send, part_recv,
        peer_send, peer_recv, sq_send, sq_recv, ac_send, ac_recv,
    ):
        feat = lax.axis_index("feat")
        row, rep = lax.axis_index("row"), lax.axis_index("rep")
        far_x = lax.div(feat, 2 * nz)
        z = lax.rem(lax.div(feat, 2), nz)
        core = lax.rem(feat, 2)
        k = row * reps + rep

        def chip(far, where):
            x = lax.rem(far_x + far, 2)
            return (x * (2 * nz) + lax.rem(where + 2 * nz, nz) * 2 + core, row, rep)

        other_core = (feat + 1 - 2 * core, row, rep)

        def peer(j):
            p = lax.rem(k + j, peers)
            return (feat, lax.div(p, reps), lax.rem(p, reps))

        loads = [
            pltpu.make_async_copy(src, dst, load_sem.at[i])
            for i, (src, dst) in enumerate(
                ((dec_hbm, dec), (enc_hbm, enc), (first_hbm, first), (second_hbm, second))
            )
        ]
        for load in loads:
            load.start()

        barrier = pltpu.get_barrier_semaphore()

        def greet(device):
            pl.semaphore_signal(barrier, inc=1, device_id=device, device_id_type=MESH)

        def far_first(j):
            m = jnp.where(core == 0, j, per_chip - 1 - j)
            return m, m != per_core

        @pl.loop(0, per_core)
        def _(j):
            m, remote = far_first(j)

            @pl.when(remote)
            def _():
                greet(chip(0, z + window * (per_core - m)))
                greet(chip(0, z - window * (per_core - m)))

        beside = sorted({(far, side * near[w]) for far, w in around for side in (1, -1)})
        for far, offset in beside:
            greet(chip(far, z + offset))
        greet(other_core)

        @pl.loop(1, peers)
        def _(j):
            greet(peer(j))

        act_send[...] = act_ref[...]
        loads[0].wait()
        wide = dec[...].astype(F32)
        square = wide * wide
        high = square.astype(BF16)
        rest = (square - high.astype(F32)).astype(BF16)
        ones = jnp.ones((8, width), BF16)
        squares_out[...] = jnp.dot(ones, high, preferred_element_type=F32) + jnp.dot(
            ones, rest, preferred_element_type=F32
        )
        pl.semaphore_wait(barrier, 2 * per_core - 2 * core + len(beside) + peers)

        def pair(src, dst, i, device):
            return pltpu.make_async_remote_copy(
                src_ref=src, dst_ref=dst, send_sem=pair_send.at[i], recv_sem=pair_recv.at[i],
                device_id=device, device_id_type=MESH,
            )

        def square_copy(j):
            return pltpu.make_async_remote_copy(
                src_ref=squares_out, dst_ref=squares_in.at[j], send_sem=sq_send.at[j], recv_sem=sq_recv.at[j],
                device_id=peer(j), device_id_type=MESH,
            )

        swap = pair(act_send, act_recv, 0, other_core)
        swap.start()
        swap.wait()
        own, his = act_send[...].astype(F32), act_recv[...].astype(F32)
        acts[0:local_rows] = jnp.where(core == 0, own, his)
        acts[local_rows:] = jnp.where(core == 0, his, own)
        block[...] = (acts[...] - dbias_ref[...].reshape(1, width)).astype(BF16)

        def each_far(action):
            @pl.loop(0, per_core)
            def _(j):
                m, remote = far_first(j)

                @pl.when(remote)
                def _():
                    action(m)

        def each_mine(action):
            @pl.loop(0, per_core)
            def _(i):
                action(core * per_core + i)

        mine = pl.ds(core * per_core, per_core)

        def gather(src, buffer, z_sems, x_sems, core_sems, between):
            def z_copy(m):
                return pltpu.make_async_remote_copy(
                    src_ref=src, dst_ref=buffer.at[0, 0, m], send_sem=z_sems[0].at[m], recv_sem=z_sems[1].at[m],
                    device_id=chip(0, z + window * (per_core - m)), device_id_type=MESH,
                )

            def beside_copy(far, w, m):
                i = (far * window + w) * per_chip + m
                return pltpu.make_async_remote_copy(
                    src_ref=buffer.at[0, 0, m], dst_ref=buffer.at[far, w, m],
                    send_sem=x_sems[0].at[i], recv_sem=x_sems[1].at[i],
                    device_id=chip(far, z + near[w]), device_id_type=MESH,
                )

            def core_copy(far, w):
                return pltpu.make_async_remote_copy(
                    src_ref=buffer.at[far, w, mine], dst_ref=buffer.at[far, w, mine],
                    send_sem=core_sems[0].at[far * window + w], recv_sem=core_sems[1].at[far * window + w],
                    device_id=other_core, device_id_type=MESH,
                )

            each_far(lambda m: z_copy(m).start())

            @pl.when(core == 1)
            def _():
                buffer[0, 0, per_core] = src[...]

            between()

            @pl.loop(0, per_core)
            def _(i):
                m, remote = far_first(per_core - 1 - i)

                @pl.when(remote)
                def _():
                    z_copy(m).wait_recv()

                for far, w in around:
                    beside_copy(far, w, m).start()

            core_copy(0, 0).start()

            def arrive(far):
                for w in range(window):
                    if (far, w) != (0, 0):
                        each_mine(lambda m: beside_copy(far, w, m).wait_recv())
                        core_copy(far, w).start()
                for w in range(window):
                    core_copy(far, w).wait_recv()

            def finish():
                each_far(lambda m: z_copy(m).wait_send())
                for far, w in around:
                    each_mine(lambda m: beside_copy(far, w, m).wait_send())
                    core_copy(far, w).wait_send()
                core_copy(0, 0).wait_send()

            return arrive, finish

        def during_first():
            @pl.loop(1, peers)
            def _(j):
                square_copy(j).start()

            loads[1].wait()

        arrive, finish_first = gather(
            block, gathered, (z_send, z_recv), (x_send, x_recv), (c_send, c_recv), during_first
        )

        def sum_copy(j, who):
            p = lax.rem(k + j, peers)
            return p, pltpu.make_async_remote_copy(
                src_ref=sums_out.at[p, who], dst_ref=sums_in.at[j, who],
                send_sem=peer_send.at[2 * j + who], recv_sem=peer_recv.at[2 * j + who],
                device_id=peer(j), device_id_type=MESH,
            )

        halves = (1 - core, core)

        def encode(far):
            rows_in = gathered[far].reshape(half_rows, width)
            value = jnp.dot(rows_in, enc[...], preferred_element_type=F32).reshape(window, 2, core_rows, feats)
            partial[far * window : (far + 1) * window] = value
            sums_out[far * window : (far + 1) * window] = value.astype(BF16)
            for who in halves:

                @pl.loop(1, peers)
                def _(j):
                    p, copy = sum_copy(j, who)

                    @pl.when(lax.div(p, window) == far)
                    def _():
                        copy.start()

        arrive(0)
        encode(0)
        arrive(1)
        encode(1)

        def active_copy(j, who):
            return pltpu.make_async_remote_copy(
                src_ref=active.at[k, who], dst_ref=active.at[k, who],
                send_sem=ac_send.at[2 * j + who], recv_sem=ac_recv.at[2 * j + who],
                device_id=peer(j), device_id_type=MESH,
            )

        for who in halves:
            pre_sum = partial[k, who] + ebias_ref[...].reshape(1, feats)
            for j in range(1, peers):
                sum_copy(j, who)[1].wait_recv()
                pre_sum += sums_in[j, who].astype(F32)
            active[k, who] = jnp.maximum(pre_sum, 0.0).astype(BF16)

            @pl.loop(1, peers)
            def _(j):
                active_copy(j, who).start()

        def wait_active(far, who):
            @pl.loop(1, peers)
            def _(j):
                @pl.when(lax.div(lax.rem(k - j + peers, peers), window) == far)
                def _():
                    active_copy(j, who).wait_recv()

        def decode(far, who):
            value = lax.dot_general(
                active[far * window : (far + 1) * window, who].reshape(window * core_rows, feats),
                dec[...], (((1,), (1,)), ((), ())), preferred_element_type=F32,
            )
            product[far, who] = value.reshape(window, core_rows, width)

        core_parts = [pair(product.at[far, 1 - core], core_in.at[far], 1 + far, other_core) for far in (0, 1)]

        def part_copy(far, w, place):
            i = (far * window + w) * per_core + place
            return pltpu.make_async_remote_copy(
                src_ref=parts_out.at[far, w, place], dst_ref=parts_in.at[far * window + w, place],
                send_sem=part_send.at[i], recv_sem=part_recv.at[i],
                device_id=chip(far, z - near[w]), device_id_type=MESH,
            )

        def place_of(j):
            return jnp.where(core == 0, j, per_core - 1 - j)

        def hand_out(far):
            core_parts[far].wait_recv()
            both_cores = product[far, core] + core_in[far]
            both_cores = both_cores.reshape(window, per_core, chip_rows, width)
            parts_out[far] = both_cores.astype(BF16)

            @pl.loop(0, per_core)
            def _(j):
                for other, w in around:
                    if other == far:
                        part_copy(far, w, place_of(j)).start()

            return both_cores

        wait_active(0, 1 - core)
        decode(0, 1 - core)
        core_parts[0].start()
        wait_active(1, 1 - core)
        decode(1, 1 - core)
        core_parts[1].start()
        wait_active(0, core)
        decode(0, core)
        own_part[...] = hand_out(0)[0]
        wait_active(1, core)
        decode(1, core)
        hand_out(1)

        def back_copy(m):
            place = m - core * per_core
            return pltpu.make_async_remote_copy(
                src_ref=z_out.at[place], dst_ref=z_in.at[place], send_sem=zr_send.at[m], recv_sem=zr_recv.at[m],
                device_id=chip(0, z + window * (m - per_core)), device_id_type=MESH,
            )

        @pl.loop(0, per_core)
        def _(j):
            place = place_of(j)
            value = own_part[place]
            for far, w in reversed(around):
                part_copy(far, w, place).wait_recv()
                value += parts_in[far * window + w, place].astype(F32)
            z_out[place] = value.astype(BF16)
            m, remote = far_first(j)

            @pl.when(remote)
            def _():
                back_copy(m).start()

        @pl.when(core == 1)
        def _():
            z_in[0] = z_out[0]

        flat = active[...].reshape(total_rows, feats)
        counts = jnp.dot(jnp.ones((8, total_rows), BF16), flat, preferred_element_type=F32)
        sum_squares = squares_out[...]
        for j in range(1, peers):
            square_copy(j).wait_recv()
            sum_squares += squares_in[j]
        norm = jnp.sqrt(sum_squares[0:1] + norm_eps)
        coef[...] = sparsity_coef / total_rows * counts[0:1] / norm

        each_far(lambda m: back_copy(m).wait_recv())
        total_out[...] = jnp.sum(z_in[...].astype(F32), axis=0)
        both = pair(total_out, total_in, 3, other_core)
        both.start()
        both.wait_recv()
        rebuilt = total_out[...] + total_in[...] + dbias_ref[...].reshape(1, width)
        recon_ref[...] = jnp.where(core == 0, rebuilt[0:local_rows], rebuilt[local_rows:]).astype(BF16)
        block_two[...] = (rebuilt - acts[...]).astype(BF16)

        def during_last():
            loads[2].wait()
            loads[3].wait()

        arrive, finish_last = gather(
            block_two, residuals, (za_send, za_recv), (xa_send, xa_recv), (ca_send, ca_recv), during_last
        )

        def turn(far):
            residual_t[:, far * half_rows : (far + 1) * half_rows] = residuals[far].reshape(half_rows, width).T

        arrive(0)
        turn(0)
        slope[...] = jnp.dot(
            residual_t[:, :half_rows], active[:window].reshape(half_rows, feats), preferred_element_type=F32
        )
        arrive(1)
        turn(1)

        part = width // 4

        def store(i):
            where = pl.ds(i * part, part)
            return pltpu.make_async_copy(step.at[where], step_hbm.at[where], store_sem.at[i])

        for i in range(4):
            where = slice(i * part, (i + 1) * part)
            slope_rest = jnp.dot(
                residual_t[where, half_rows:], active[window:].reshape(half_rows, feats),
                preferred_element_type=F32,
            )
            gradient = 2.0 / total_rows * (slope[where] + slope_rest) + coef[...] * dec[where].astype(F32)
            moment_one = beta_one * first[where].astype(F32) + (1.0 - beta_one) * gradient
            moment_two = beta_two * second[where].astype(F32) + (1.0 - beta_two) * gradient * gradient
            step[where] = (
                moment_one * (1.0 / bias_one) / (jnp.sqrt(moment_two * (1.0 / bias_two)) + adam_eps)
            ).astype(BF16)
            store(i).start()

        finish_first()
        finish_last()
        each_far(lambda m: back_copy(m).wait_send())
        for copy in (*core_parts, both):
            copy.wait_send()

        @pl.loop(0, per_core)
        def _(j):
            for far, w in around:
                part_copy(far, w, j).wait_send()

        @pl.loop(1, peers)
        def _(j):
            square_copy(j).wait_send()
            for who in (0, 1):
                sum_copy(j, who)[1].wait_send()
                active_copy(j, who).wait_send()

        for i in range(4):
            store(i).wait()

    scratch = [
        *(pltpu.VMEM((width, feats), BF16) for _ in range(5)),
        pltpu.SemaphoreType.DMA((4,)),
        pltpu.SemaphoreType.DMA((4,)),
        pltpu.VMEM((local_rows, width), BF16),
        pltpu.VMEM((local_rows, width), BF16),
        pltpu.VMEM((chip_rows, width), F32),
        pltpu.VMEM((2, window, per_chip, chip_rows, width), BF16),
        pltpu.VMEM((chip_rows, width), BF16),
        pltpu.VMEM((peers, 2, core_rows, feats), F32),
        *(pltpu.VMEM((peers, 2, core_rows, feats), BF16) for _ in range(3)),
        pltpu.VMEM((8, feats), F32),
        pltpu.VMEM((peers, 8, feats), F32),
        pltpu.VMEM((2, 2, window, core_rows, width), F32),
        pltpu.VMEM((2, window, core_rows, width), F32),
        pltpu.VMEM((2, window, per_core, chip_rows, width), BF16),
        pltpu.VMEM((2 * window, per_core, chip_rows, width), BF16),
        pltpu.VMEM((per_core, chip_rows, width), F32),
        pltpu.VMEM((per_core, chip_rows, width), BF16),
        pltpu.VMEM((per_core, chip_rows, width), BF16),
        pltpu.VMEM((chip_rows, width), F32),
        pltpu.VMEM((chip_rows, width), F32),
        pltpu.VMEM((2, window, per_chip, chip_rows, width), BF16),
        pltpu.VMEM((chip_rows, width), BF16),
        pltpu.VMEM((1, feats), F32),
        pltpu.VMEM((width, total_rows), BF16),
        pltpu.VMEM((width, feats), F32),
        *(pltpu.SemaphoreType.DMA((4,)) for _ in range(2)),
        *(pltpu.SemaphoreType.DMA((per_chip,)) for _ in range(6)),
        *(pltpu.SemaphoreType.DMA((2 * window * per_chip,)) for _ in range(4)),
        *(pltpu.SemaphoreType.DMA((2 * window,)) for _ in range(4)),
        *(pltpu.SemaphoreType.DMA((2 * window * per_core,)) for _ in range(2)),
        *(pltpu.SemaphoreType.DMA((2 * peers,)) for _ in range(2)),
        *(pltpu.SemaphoreType.DMA((peers,)) for _ in range(2)),
        *(pltpu.SemaphoreType.DMA((2 * peers,)) for _ in range(2)),
    ]
    return kernel, scratch


def shards(nz, rows, reps, activations, enc_weight, enc_bias, dec_weight, dec_bias, first_moment, second_moment):
    local_rows, width = activations.shape
    feats = enc_weight.shape[1]
    kernel, scratch = make_kernel(nz, rows, reps, local_rows, width, feats)
    vmem = pl.BlockSpec(memory_space=pltpu.VMEM)
    hbm = pl.BlockSpec(memory_space=pl.ANY)
    recon, step = pl.pallas_call(
        kernel,
        out_shape=(
            jax.ShapeDtypeStruct((local_rows, width), BF16),
            jax.ShapeDtypeStruct((width, feats), BF16),
        ),
        in_specs=[vmem, hbm, vmem, hbm, vmem, hbm, hbm],
        out_specs=(vmem, hbm),
        scratch_shapes=scratch,
        compiler_params=pltpu.CompilerParams(
            collective_id=0, has_side_effects=True, vmem_limit_bytes=53 * 2**20
        ),
    )(activations, enc_weight, enc_bias, dec_weight.T, dec_bias, first_moment.T, second_moment.T)
    return recon, step.T


def solution(mesh):
    nz, rows, reps = mesh.shape["feat"] // 4, mesh.shape["row"], mesh.shape["rep"]

    def step(*args):
        return shards(nz, rows, reps, *args)

    return jax.shard_map(
        step,
        mesh=mesh,
        in_specs=(
            P("feat", ("row", "rep")),
            P(("row", "rep"), "feat"),
            P("feat"),
            P("feat", ("row", "rep")),
            P(("row", "rep")),
            P("feat", ("row", "rep")),
            P("feat", ("row", "rep")),
        ),
        out_specs=(P("feat", ("row", "rep")), P("feat", ("row", "rep"))),
        check_vma=False,
    )
```

```python
import jax
import jax.numpy as jnp
from jax import lax
from jax.experimental import pallas as pl
from jax.experimental.pallas import tpu as pltpu
from jax.sharding import PartitionSpec as P

sparsity_coef = 5.0
beta_one = 0.9
beta_two = 0.999
bias_one = 0.99997344
bias_two = 0.095207853
adam_eps = 1e-08
norm_eps = 1e-06

MESH = pl.DeviceIdType.MESH
F32 = jnp.float32
BF16 = jnp.bfloat16


def make_kernel(nz, rows, reps, local_rows, width, feats):
    near = (0, 1, 2, -1)
    window = len(near)
    per_chip = nz // window
    per_core = per_chip // 2
    chip_rows = 2 * local_rows
    total_rows = 2 * nz * chip_rows
    half_rows = total_rows // 2
    peers = rows * reps
    group = total_rows // peers
    core_rows = per_core * chip_rows
    assert peers == 2 * window and group == 2 * core_rows
    around = [(far, w) for far in (1, 0) for w in range(window) if (far, w) != (0, 0)]

    def kernel(
        act_ref, enc_hbm, ebias_ref, dec_hbm, dbias_ref, first_hbm, second_hbm,
        recon_ref, step_hbm,
        enc, dec, first, second, step, load_sem, store_sem,
        act_send, act_recv, acts, gathered, block, partial, sums_out, sums_in, active,
        squares_out, squares_in, product, core_in, parts_out, parts_in, own_part, z_out, z_in, total_out, total_in, residuals,
        block_two, coef, residual_t, slope,
        pair_send, pair_recv, z_send, z_recv, zr_send, zr_recv, za_send, za_recv,
        x_send, x_recv, xa_send, xa_recv, c_send, c_recv, ca_send, ca_recv, part_send, part_recv,
        peer_send, peer_recv, sq_send, sq_recv, ac_send, ac_recv,
    ):
        feat = lax.axis_index("feat")
        row, rep = lax.axis_index("row"), lax.axis_index("rep")
        far_x = lax.div(feat, 2 * nz)
        z = lax.rem(lax.div(feat, 2), nz)
        core = lax.rem(feat, 2)
        k = row * reps + rep

        def chip(far, where):
            x = lax.rem(far_x + far, 2)
            return (x * (2 * nz) + lax.rem(where + 2 * nz, nz) * 2 + core, row, rep)

        other_core = (feat + 1 - 2 * core, row, rep)

        def peer(j):
            p = lax.rem(k + j, peers)
            return (feat, lax.div(p, reps), lax.rem(p, reps))

        loads = [
            pltpu.make_async_copy(src, dst, load_sem.at[i])
            for i, (src, dst) in enumerate(
                ((dec_hbm, dec), (enc_hbm, enc), (first_hbm, first), (second_hbm, second))
            )
        ]
        for load in loads:
            load.start()

        barrier = pltpu.get_barrier_semaphore()

        def greet(device):
            pl.semaphore_signal(barrier, inc=1, device_id=device, device_id_type=MESH)

        def far_first(j):
            return jnp.where(core == 0, j, per_chip - 1 - j)

        def away(m):
            return window * (m - per_core) + window // 2

        @pl.loop(0, per_core)
        def _(j):
            greet(chip(0, z + away(far_first(j))))
            greet(chip(0, z - away(far_first(j))))

        beside = sorted({(far, side * near[w]) for far, w in around for side in (1, -1)})
        for far, offset in beside:
            greet(chip(far, z + offset))
        greet(other_core)

        @pl.loop(1, peers)
        def _(j):
            greet(peer(j))

        act_send[...] = act_ref[...]
        loads[0].wait()
        wide = dec[...].astype(F32)
        square = wide * wide
        high = square.astype(BF16)
        rest = (square - high.astype(F32)).astype(BF16)
        ones = jnp.ones((8, width), BF16)
        squares_out[...] = jnp.dot(ones, high, preferred_element_type=F32) + jnp.dot(
            ones, rest, preferred_element_type=F32
        )
        pl.semaphore_wait(barrier, 2 * per_core + len(beside) + peers)

        def pair(src, dst, i, device):
            return pltpu.make_async_remote_copy(
                src_ref=src, dst_ref=dst, send_sem=pair_send.at[i], recv_sem=pair_recv.at[i],
                device_id=device, device_id_type=MESH,
            )

        def square_copy(j):
            return pltpu.make_async_remote_copy(
                src_ref=squares_out, dst_ref=squares_in.at[j], send_sem=sq_send.at[j], recv_sem=sq_recv.at[j],
                device_id=peer(j), device_id_type=MESH,
            )

        swap = pair(act_send, act_recv, 0, other_core)
        swap.start()
        swap.wait()
        own, his = act_send[...].astype(F32), act_recv[...].astype(F32)
        acts[0:local_rows] = jnp.where(core == 0, own, his)
        acts[local_rows:] = jnp.where(core == 0, his, own)
        block[...] = (acts[...] - dbias_ref[...].reshape(1, width)).astype(BF16)

        def each_far(action):
            @pl.loop(0, per_core)
            def _(j):
                action(far_first(j))

        def each_mine(action):
            @pl.loop(0, per_core)
            def _(i):
                action(core * per_core + i)

        mine = pl.ds(core * per_core, per_core)

        def gather(src, buffer, z_sems, x_sems, core_sems, between):
            def z_copy(m):
                return pltpu.make_async_remote_copy(
                    src_ref=src, dst_ref=buffer.at[0, 0, m], send_sem=z_sems[0].at[m], recv_sem=z_sems[1].at[m],
                    device_id=chip(0, z - away(m)), device_id_type=MESH,
                )

            def beside_copy(far, w, m):
                i = (far * window + w) * per_chip + m
                return pltpu.make_async_remote_copy(
                    src_ref=buffer.at[0, 0, m], dst_ref=buffer.at[far, w, m],
                    send_sem=x_sems[0].at[i], recv_sem=x_sems[1].at[i],
                    device_id=chip(far, z + near[w]), device_id_type=MESH,
                )

            def core_copy(far, w):
                return pltpu.make_async_remote_copy(
                    src_ref=buffer.at[far, w, mine], dst_ref=buffer.at[far, w, mine],
                    send_sem=core_sems[0].at[far * window + w], recv_sem=core_sems[1].at[far * window + w],
                    device_id=other_core, device_id_type=MESH,
                )

            each_far(lambda m: z_copy(m).start())

            between()

            @pl.loop(0, per_core)
            def _(i):
                m = far_first(per_core - 1 - i)
                z_copy(m).wait_recv()
                for far, w in around:
                    beside_copy(far, w, m).start()

            core_copy(0, 0).start()

            def arrive(far):
                for w in range(window):
                    if (far, w) != (0, 0):
                        each_mine(lambda m: beside_copy(far, w, m).wait_recv())
                        core_copy(far, w).start()
                for w in range(window):
                    core_copy(far, w).wait_recv()

            def finish_beside():
                each_far(lambda m: z_copy(m).wait_send())
                for far, w in around:
                    each_mine(lambda m: beside_copy(far, w, m).wait_send())

            def finish_core():
                for i in range(2 * window):
                    core_copy(i // window, i % window).wait_send()

            return arrive, finish_beside, finish_core

        def during_first():
            @pl.loop(1, peers)
            def _(j):
                square_copy(j).start()

            loads[1].wait()

        arrive, finish_beside, finish_core = gather(
            block, gathered, (z_send, z_recv), (x_send, x_recv), (c_send, c_recv), during_first
        )

        def sum_copy(j, who):
            p = lax.rem(k + j, peers)
            return p, pltpu.make_async_remote_copy(
                src_ref=sums_out.at[p, who], dst_ref=sums_in.at[j, who],
                send_sem=peer_send.at[2 * j + who], recv_sem=peer_recv.at[2 * j + who],
                device_id=peer(j), device_id_type=MESH,
            )

        halves = (1 - core, core)

        def encode(far):
            rows_in = gathered[far].reshape(half_rows, width)
            value = jnp.dot(rows_in, enc[...], preferred_element_type=F32).reshape(window, 2, core_rows, feats)
            partial[far * window : (far + 1) * window] = value
            sums_out[far * window : (far + 1) * window] = value.astype(BF16)
            for who in halves:

                @pl.loop(1, peers)
                def _(j):
                    p, copy = sum_copy(j, who)

                    @pl.when(lax.div(p, window) == far)
                    def _():
                        copy.start()

        arrive(0)
        encode(0)
        arrive(1)
        encode(1)

        def active_copy(j, who):
            return pltpu.make_async_remote_copy(
                src_ref=active.at[k, who], dst_ref=active.at[k, who],
                send_sem=ac_send.at[2 * j + who], recv_sem=ac_recv.at[2 * j + who],
                device_id=peer(j), device_id_type=MESH,
            )

        for who in halves:
            pre_sum = partial[k, who] + ebias_ref[...].reshape(1, feats)
            for j in range(1, peers):
                sum_copy(j, who)[1].wait_recv()
                pre_sum += sums_in[j, who].astype(F32)
            active[k, who] = jnp.maximum(pre_sum, 0.0).astype(BF16)

            @pl.loop(1, peers)
            def _(j):
                active_copy(j, who).start()

        def wait_active(far, who):
            @pl.loop(1, peers)
            def _(j):
                @pl.when(lax.div(lax.rem(k - j + peers, peers), window) == far)
                def _():
                    active_copy(j, who).wait_recv()

        def decode(far, who):
            value = lax.dot_general(
                active[far * window : (far + 1) * window, who].reshape(window * core_rows, feats),
                dec[...], (((1,), (1,)), ((), ())), preferred_element_type=F32,
            )
            product[far, who] = value.reshape(window, core_rows, width)

        core_parts = [pair(product.at[far, 1 - core], core_in.at[far], 1 + far, other_core) for far in (0, 1)]

        def part_copy(far, w, place):
            i = (far * window + w) * per_core + place
            return pltpu.make_async_remote_copy(
                src_ref=parts_out.at[far, w, place], dst_ref=parts_in.at[far * window + w, place],
                send_sem=part_send.at[i], recv_sem=part_recv.at[i],
                device_id=chip(far, z - near[w]), device_id_type=MESH,
            )

        def place_of(j):
            return jnp.where(core == 0, j, per_core - 1 - j)

        def hand_out(far):
            core_parts[far].wait_recv()
            both_cores = product[far, core] + core_in[far]
            both_cores = both_cores.reshape(window, per_core, chip_rows, width)
            parts_out[far] = both_cores.astype(BF16)

            @pl.loop(0, per_core)
            def _(j):
                for other, w in around:
                    if other == far:
                        part_copy(far, w, place_of(j)).start()

            return both_cores

        wait_active(0, 1 - core)
        decode(0, 1 - core)
        core_parts[0].start()
        wait_active(1, 1 - core)
        decode(1, 1 - core)
        core_parts[1].start()
        wait_active(0, core)
        decode(0, core)
        own_part[...] = hand_out(0)[0]
        wait_active(1, core)
        decode(1, core)
        hand_out(1)

        def back_copy(m):
            place = m - core * per_core
            return pltpu.make_async_remote_copy(
                src_ref=z_out.at[place], dst_ref=z_in.at[place], send_sem=zr_send.at[m], recv_sem=zr_recv.at[m],
                device_id=chip(0, z + away(m)), device_id_type=MESH,
            )

        @pl.loop(0, per_core)
        def _(j):
            place = place_of(j)
            value = own_part[place]
            for far, w in reversed(around):
                part_copy(far, w, place).wait_recv()
                value += parts_in[far * window + w, place].astype(F32)
            z_out[place] = value.astype(BF16)
            back_copy(far_first(j)).start()

        flat = active[...].reshape(total_rows, feats)
        counts = jnp.dot(jnp.ones((8, total_rows), BF16), flat, preferred_element_type=F32)
        sum_squares = squares_out[...]
        for j in range(1, peers):
            square_copy(j).wait_recv()
            sum_squares += squares_in[j]
        norm = jnp.sqrt(sum_squares[0:1] + norm_eps)
        coef[...] = sparsity_coef / total_rows * counts[0:1] / norm

        each_far(lambda m: back_copy(m).wait_recv())
        total_out[...] = jnp.sum(z_in[...].astype(F32), axis=0)
        both = pair(total_out, total_in, 3, other_core)
        both.start()
        both.wait_recv()
        rebuilt = total_out[...] + total_in[...] + dbias_ref[...].reshape(1, width)
        recon_ref[...] = jnp.where(core == 0, rebuilt[0:local_rows], rebuilt[local_rows:]).astype(BF16)
        block_two[...] = (rebuilt - acts[...]).astype(BF16)

        def during_last():
            loads[2].wait()
            loads[3].wait()
            finish_beside()
            finish_core()
            each_far(lambda m: back_copy(m).wait_send())
            for copy in (*core_parts, both):
                copy.wait_send()

            @pl.loop(0, per_core)
            def _(j):
                for far, w in around:
                    part_copy(far, w, j).wait_send()

            @pl.loop(1, peers)
            def _(j):
                square_copy(j).wait_send()
                for who in (0, 1):
                    sum_copy(j, who)[1].wait_send()
                    active_copy(j, who).wait_send()


        arrive, finish_beside_last, finish_core_last = gather(
            block_two, residuals, (za_send, za_recv), (xa_send, xa_recv), (ca_send, ca_recv), during_last
        )

        def turn(far):
            residual_t[:, far * half_rows : (far + 1) * half_rows] = residuals[far].reshape(half_rows, width).T

        arrive(0)
        turn(0)
        slope[...] = 2.0 / total_rows * jnp.dot(
            residual_t[:, :half_rows], active[:window].reshape(half_rows, feats), preferred_element_type=F32
        ) + coef[...] * dec[...].astype(F32)
        finish_beside_last()
        arrive(1)
        turn(1)

        part = width // 4

        def store(i):
            where = pl.ds(i * part, part)
            return pltpu.make_async_copy(step.at[where], step_hbm.at[where], store_sem.at[i])

        for i in range(4):
            where = slice(i * part, (i + 1) * part)
            slope_rest = jnp.dot(
                residual_t[where, half_rows:], active[window:].reshape(half_rows, feats),
                preferred_element_type=F32,
            )
            gradient = slope[where] + 2.0 / total_rows * slope_rest
            moment_one = beta_one * first[where].astype(F32) + (1.0 - beta_one) * gradient
            moment_two = beta_two * second[where].astype(F32) + (1.0 - beta_two) * gradient * gradient
            step[where] = (
                moment_one * (1.0 / bias_one) / (jnp.sqrt(moment_two * (1.0 / bias_two)) + adam_eps)
            ).astype(BF16)
            store(i).start()

        finish_core_last()
        for i in range(4):
            store(i).wait()

    scratch = [
        *(pltpu.VMEM((width, feats), BF16) for _ in range(5)),
        pltpu.SemaphoreType.DMA((4,)),
        pltpu.SemaphoreType.DMA((4,)),
        pltpu.VMEM((local_rows, width), BF16),
        pltpu.VMEM((local_rows, width), BF16),
        pltpu.VMEM((chip_rows, width), F32),
        pltpu.VMEM((2, window, per_chip, chip_rows, width), BF16),
        pltpu.VMEM((chip_rows, width), BF16),
        pltpu.VMEM((peers, 2, core_rows, feats), F32),
        *(pltpu.VMEM((peers, 2, core_rows, feats), BF16) for _ in range(3)),
        pltpu.VMEM((8, feats), F32),
        pltpu.VMEM((peers, 8, feats), F32),
        pltpu.VMEM((2, 2, window, core_rows, width), F32),
        pltpu.VMEM((2, window, core_rows, width), F32),
        pltpu.VMEM((2, window, per_core, chip_rows, width), BF16),
        pltpu.VMEM((2 * window, per_core, chip_rows, width), BF16),
        pltpu.VMEM((per_core, chip_rows, width), F32),
        pltpu.VMEM((per_core, chip_rows, width), BF16),
        pltpu.VMEM((per_core, chip_rows, width), BF16),
        pltpu.VMEM((chip_rows, width), F32),
        pltpu.VMEM((chip_rows, width), F32),
        pltpu.VMEM((2, window, per_chip, chip_rows, width), BF16),
        pltpu.VMEM((chip_rows, width), BF16),
        pltpu.VMEM((1, feats), F32),
        pltpu.VMEM((width, total_rows), BF16),
        pltpu.VMEM((width, feats), F32),
        *(pltpu.SemaphoreType.DMA((4,)) for _ in range(2)),
        *(pltpu.SemaphoreType.DMA((per_chip,)) for _ in range(6)),
        *(pltpu.SemaphoreType.DMA((2 * window * per_chip,)) for _ in range(4)),
        *(pltpu.SemaphoreType.DMA((2 * window,)) for _ in range(4)),
        *(pltpu.SemaphoreType.DMA((2 * window * per_core,)) for _ in range(2)),
        *(pltpu.SemaphoreType.DMA((2 * peers,)) for _ in range(2)),
        *(pltpu.SemaphoreType.DMA((peers,)) for _ in range(2)),
        *(pltpu.SemaphoreType.DMA((2 * peers,)) for _ in range(2)),
    ]
    return kernel, scratch


def shards(nz, rows, reps, activations, enc_weight, enc_bias, dec_weight, dec_bias, first_moment, second_moment):
    local_rows, width = activations.shape
    feats = enc_weight.shape[1]
    kernel, scratch = make_kernel(nz, rows, reps, local_rows, width, feats)
    vmem = pl.BlockSpec(memory_space=pltpu.VMEM)
    hbm = pl.BlockSpec(memory_space=pl.ANY)
    recon, step = pl.pallas_call(
        kernel,
        out_shape=(
            jax.ShapeDtypeStruct((local_rows, width), BF16),
            jax.ShapeDtypeStruct((width, feats), BF16),
        ),
        in_specs=[vmem, hbm, vmem, hbm, vmem, hbm, hbm],
        out_specs=(vmem, hbm),
        scratch_shapes=scratch,
        compiler_params=pltpu.CompilerParams(
            collective_id=0, has_side_effects=True, vmem_limit_bytes=60 * 2**20
        ),
    )(activations, enc_weight, enc_bias, dec_weight.T, dec_bias, first_moment.T, second_moment.T)
    return recon, step.T


def solution(mesh):
    nz, rows, reps = mesh.shape["feat"] // 4, mesh.shape["row"], mesh.shape["rep"]

    def step(*args):
        return shards(nz, rows, reps, *args)

    return jax.shard_map(
        step,
        mesh=mesh,
        in_specs=(
            P("feat", ("row", "rep")),
            P(("row", "rep"), "feat"),
            P("feat"),
            P("feat", ("row", "rep")),
            P(("row", "rep")),
            P("feat", ("row", "rep")),
            P("feat", ("row", "rep")),
        ),
        out_specs=(P("feat", ("row", "rep")), P("feat", ("row", "rep"))),
        check_vma=False,
    )
```

```python
import jax
import jax.numpy as jnp
from jax import lax
from jax.experimental import pallas as pl
from jax.experimental.pallas import tpu as pltpu
from jax.sharding import PartitionSpec as P

sparsity_coef = 5.0
beta_one = 0.9
beta_two = 0.999
bias_one = 0.99997344
bias_two = 0.095207853
adam_eps = 1e-08
norm_eps = 1e-06

MESH = pl.DeviceIdType.MESH
F32 = jnp.float32
BF16 = jnp.bfloat16


def make_kernel(nz, rows, reps, local_rows, width, feats):
    near = (0, 1, 2, -1)
    window = len(near)
    per_chip = nz // window
    per_core = per_chip // 2
    chip_rows = 2 * local_rows
    total_rows = 2 * nz * chip_rows
    half_rows = total_rows // 2
    peers = rows * reps
    group = total_rows // peers
    core_rows = per_core * chip_rows
    assert peers == 2 * window and group == 2 * core_rows
    around = [(far, w) for far in (1, 0) for w in range(window) if (far, w) != (0, 0)]

    def kernel(
        act_hbm, enc_hbm, ebias_hbm, dec_hbm, dbias_hbm, first_hbm, second_hbm,
        recon_hbm, step_hbm,
        ebias_ref, dbias_ref, recon_ref, enc, dec, first, second, step, load_sem, store_sem,
        act_send, act_recv, acts, gathered, block, partial, sums_out, sums_in, active,
        squares_out, squares_in, product, core_in, parts_out, parts_in, own_part, z_out, z_in, total_out, total_in, residuals,
        block_two, coef, residual_t, slope,
        pair_send, pair_recv, z_send, z_recv, zr_send, zr_recv, za_send, za_recv,
        x_send, x_recv, xa_send, xa_recv, c_send, c_recv, ca_send, ca_recv, part_send, part_recv,
        peer_send, peer_recv, sq_send, sq_recv, ac_send, ac_recv,
    ):
        feat = lax.axis_index("feat")
        row, rep = lax.axis_index("row"), lax.axis_index("rep")
        far_x = lax.div(feat, 2 * nz)
        z = lax.rem(lax.div(feat, 2), nz)
        core = lax.rem(feat, 2)
        k = row * reps + rep

        def chip(far, where):
            x = lax.rem(far_x + far, 2)
            return (x * (2 * nz) + lax.rem(where + 2 * nz, nz) * 2 + core, row, rep)

        other_core = (feat + 1 - 2 * core, row, rep)

        def peer(j):
            p = lax.rem(k + j, peers)
            return (feat, lax.div(p, reps), lax.rem(p, reps))

        loads = [
            pltpu.make_async_copy(src, dst, load_sem.at[i])
            for i, (src, dst) in enumerate(
                (
                    (act_hbm, act_send), (dbias_hbm, dbias_ref), (dec_hbm, dec), (enc_hbm, enc),
                    (ebias_hbm, ebias_ref), (first_hbm, first), (second_hbm, second),
                )
            )
        ]
        for load in loads:
            load.start()

        barrier = pltpu.get_barrier_semaphore()

        def greet(device):
            pl.semaphore_signal(barrier, inc=1, device_id=device, device_id_type=MESH)

        def far_first(j):
            return jnp.where(core == 0, j, per_chip - 1 - j)

        def away(m):
            return window * (m - per_core) + window // 2

        @pl.loop(0, per_core)
        def _(j):
            greet(chip(0, z + away(far_first(j))))
            greet(chip(0, z - away(far_first(j))))

        beside = sorted({(far, side * near[w]) for far, w in around for side in (1, -1)})
        for far, offset in beside:
            greet(chip(far, z + offset))
        greet(other_core)

        @pl.loop(1, peers)
        def _(j):
            greet(peer(j))

        for load in loads[:3]:
            load.wait()
        wide = dec[...].astype(F32)
        square = wide * wide
        high = square.astype(BF16)
        rest = (square - high.astype(F32)).astype(BF16)
        ones = jnp.ones((8, width), BF16)
        squares_out[...] = jnp.dot(ones, high, preferred_element_type=F32) + jnp.dot(
            ones, rest, preferred_element_type=F32
        )
        pl.semaphore_wait(barrier, 2 * per_core + len(beside) + peers)

        def pair(src, dst, i, device):
            return pltpu.make_async_remote_copy(
                src_ref=src, dst_ref=dst, send_sem=pair_send.at[i], recv_sem=pair_recv.at[i],
                device_id=device, device_id_type=MESH,
            )

        def square_copy(j):
            return pltpu.make_async_remote_copy(
                src_ref=squares_out, dst_ref=squares_in.at[j], send_sem=sq_send.at[j], recv_sem=sq_recv.at[j],
                device_id=peer(j), device_id_type=MESH,
            )

        swap = pair(act_send, act_recv, 0, other_core)
        swap.start()
        swap.wait()
        own, his = act_send[...].astype(F32), act_recv[...].astype(F32)
        acts[0:local_rows] = jnp.where(core == 0, own, his)
        acts[local_rows:] = jnp.where(core == 0, his, own)
        block[...] = (acts[...] - dbias_ref[...].reshape(1, width)).astype(BF16)

        def each_far(action):
            @pl.loop(0, per_core)
            def _(j):
                action(far_first(j))

        def each_mine(action):
            @pl.loop(0, per_core)
            def _(i):
                action(core * per_core + i)

        mine = pl.ds(core * per_core, per_core)

        def gather(src, buffer, z_sems, x_sems, core_sems, between):
            def z_copy(m):
                return pltpu.make_async_remote_copy(
                    src_ref=src, dst_ref=buffer.at[0, 0, m], send_sem=z_sems[0].at[m], recv_sem=z_sems[1].at[m],
                    device_id=chip(0, z - away(m)), device_id_type=MESH,
                )

            def beside_copy(far, w, m):
                i = (far * window + w) * per_chip + m
                return pltpu.make_async_remote_copy(
                    src_ref=buffer.at[0, 0, m], dst_ref=buffer.at[far, w, m],
                    send_sem=x_sems[0].at[i], recv_sem=x_sems[1].at[i],
                    device_id=chip(far, z + near[w]), device_id_type=MESH,
                )

            def core_copy(far, w):
                return pltpu.make_async_remote_copy(
                    src_ref=buffer.at[far, w, mine], dst_ref=buffer.at[far, w, mine],
                    send_sem=core_sems[0].at[far * window + w], recv_sem=core_sems[1].at[far * window + w],
                    device_id=other_core, device_id_type=MESH,
                )

            each_far(lambda m: z_copy(m).start())

            between()

            @pl.loop(0, per_core)
            def _(i):
                m = far_first(per_core - 1 - i)
                z_copy(m).wait_recv()
                for far, w in around:
                    beside_copy(far, w, m).start()

            core_copy(0, 0).start()

            def arrive(far):
                for w in range(window):
                    if (far, w) != (0, 0):
                        each_mine(lambda m: beside_copy(far, w, m).wait_recv())
                        core_copy(far, w).start()
                for w in range(window):
                    core_copy(far, w).wait_recv()

            def finish_beside():
                each_far(lambda m: z_copy(m).wait_send())
                for far, w in around:
                    each_mine(lambda m: beside_copy(far, w, m).wait_send())

            def finish_core():
                for i in range(2 * window):
                    core_copy(i // window, i % window).wait_send()

            return arrive, finish_beside, finish_core

        def during_first():
            @pl.loop(1, peers)
            def _(j):
                square_copy(j).start()

            loads[3].wait()
            loads[4].wait()

        arrive, finish_beside, finish_core = gather(
            block, gathered, (z_send, z_recv), (x_send, x_recv), (c_send, c_recv), during_first
        )

        def sum_copy(j, who):
            p = lax.rem(k + j, peers)
            return p, pltpu.make_async_remote_copy(
                src_ref=sums_out.at[p, who], dst_ref=sums_in.at[j, who],
                send_sem=peer_send.at[2 * j + who], recv_sem=peer_recv.at[2 * j + who],
                device_id=peer(j), device_id_type=MESH,
            )

        halves = (1 - core, core)

        def encode(far):
            rows_in = gathered[far].reshape(half_rows, width)
            value = jnp.dot(rows_in, enc[...], preferred_element_type=F32).reshape(window, 2, core_rows, feats)
            partial[far * window : (far + 1) * window] = value
            sums_out[far * window : (far + 1) * window] = value.astype(BF16)
            for who in halves:

                @pl.loop(1, peers)
                def _(j):
                    p, copy = sum_copy(j, who)

                    @pl.when(lax.div(p, window) == far)
                    def _():
                        copy.start()

        arrive(0)
        encode(0)
        arrive(1)
        encode(1)

        def active_copy(j, who):
            return pltpu.make_async_remote_copy(
                src_ref=active.at[k, who], dst_ref=active.at[k, who],
                send_sem=ac_send.at[2 * j + who], recv_sem=ac_recv.at[2 * j + who],
                device_id=peer(j), device_id_type=MESH,
            )

        for who in halves:
            pre_sum = partial[k, who] + ebias_ref[...].reshape(1, feats)
            for j in range(1, peers):
                sum_copy(j, who)[1].wait_recv()
                pre_sum += sums_in[j, who].astype(F32)
            active[k, who] = jnp.maximum(pre_sum, 0.0).astype(BF16)

            @pl.loop(1, peers)
            def _(j):
                active_copy(j, who).start()

        def wait_active(far, who):
            @pl.loop(1, peers)
            def _(j):
                @pl.when(lax.div(lax.rem(k - j + peers, peers), window) == far)
                def _():
                    active_copy(j, who).wait_recv()

        def decode(far, who):
            value = lax.dot_general(
                active[far * window : (far + 1) * window, who].reshape(window * core_rows, feats),
                dec[...], (((1,), (1,)), ((), ())), preferred_element_type=F32,
            )
            product[far, who] = value.reshape(window, core_rows, width)

        core_parts = [pair(product.at[far, 1 - core], core_in.at[far], 1 + far, other_core) for far in (0, 1)]

        def part_copy(far, w, place):
            i = (far * window + w) * per_core + place
            return pltpu.make_async_remote_copy(
                src_ref=parts_out.at[far, w, place], dst_ref=parts_in.at[far * window + w, place],
                send_sem=part_send.at[i], recv_sem=part_recv.at[i],
                device_id=chip(far, z - near[w]), device_id_type=MESH,
            )

        def place_of(j):
            return jnp.where(core == 0, j, per_core - 1 - j)

        def hand_out(far):
            core_parts[far].wait_recv()
            both_cores = product[far, core] + core_in[far]
            both_cores = both_cores.reshape(window, per_core, chip_rows, width)
            parts_out[far] = both_cores.astype(BF16)

            @pl.loop(0, per_core)
            def _(j):
                for other, w in around:
                    if other == far:
                        part_copy(far, w, place_of(j)).start()

            return both_cores

        wait_active(0, 1 - core)
        decode(0, 1 - core)
        core_parts[0].start()
        wait_active(1, 1 - core)
        decode(1, 1 - core)
        core_parts[1].start()
        wait_active(0, core)
        decode(0, core)
        own_part[...] = hand_out(0)[0]
        wait_active(1, core)
        decode(1, core)
        hand_out(1)

        def back_copy(m):
            place = m - core * per_core
            return pltpu.make_async_remote_copy(
                src_ref=z_out.at[place], dst_ref=z_in.at[place], send_sem=zr_send.at[m], recv_sem=zr_recv.at[m],
                device_id=chip(0, z + away(m)), device_id_type=MESH,
            )

        @pl.loop(0, per_core)
        def _(j):
            place = place_of(j)
            value = own_part[place]
            for far, w in reversed(around):
                part_copy(far, w, place).wait_recv()
                value += parts_in[far * window + w, place].astype(F32)
            z_out[place] = value.astype(BF16)
            back_copy(far_first(j)).start()

        flat = active[...].reshape(total_rows, feats)
        counts = jnp.dot(jnp.ones((8, total_rows), BF16), flat, preferred_element_type=F32)
        sum_squares = squares_out[...]
        for j in range(1, peers):
            square_copy(j).wait_recv()
            sum_squares += squares_in[j]
        norm = jnp.sqrt(sum_squares[0:1] + norm_eps)
        coef[...] = sparsity_coef / total_rows * counts[0:1] / norm

        each_far(lambda m: back_copy(m).wait_recv())
        total_out[...] = jnp.sum(z_in[...].astype(F32), axis=0)
        both = pair(total_out, total_in, 3, other_core)
        both.start()
        both.wait_recv()
        rebuilt = total_out[...] + total_in[...] + dbias_ref[...].reshape(1, width)
        recon_ref[...] = jnp.where(core == 0, rebuilt[0:local_rows], rebuilt[local_rows:]).astype(BF16)
        store_recon = pltpu.make_async_copy(recon_ref, recon_hbm, store_sem.at[4])
        store_recon.start()
        block_two[...] = (rebuilt - acts[...]).astype(BF16)

        def during_last():
            loads[5].wait()
            loads[6].wait()
            store_recon.wait()
            finish_beside()
            finish_core()
            each_far(lambda m: back_copy(m).wait_send())
            for copy in (*core_parts, both):
                copy.wait_send()

            @pl.loop(0, per_core)
            def _(j):
                for far, w in around:
                    part_copy(far, w, j).wait_send()

            @pl.loop(1, peers)
            def _(j):
                square_copy(j).wait_send()
                for who in (0, 1):
                    sum_copy(j, who)[1].wait_send()
                    active_copy(j, who).wait_send()


        arrive, finish_beside_last, finish_core_last = gather(
            block_two, residuals, (za_send, za_recv), (xa_send, xa_recv), (ca_send, ca_recv), during_last
        )

        def turn(far):
            residual_t[:, far * half_rows : (far + 1) * half_rows] = residuals[far].reshape(half_rows, width).T

        arrive(0)
        turn(0)
        slope[...] = 2.0 / total_rows * jnp.dot(
            residual_t[:, :half_rows], active[:window].reshape(half_rows, feats), preferred_element_type=F32
        ) + coef[...] * dec[...].astype(F32)
        finish_beside_last()
        arrive(1)
        turn(1)

        part = width // 4

        def store(i):
            where = pl.ds(i * part, part)
            return pltpu.make_async_copy(step.at[where], step_hbm.at[where], store_sem.at[i])

        for i in range(4):
            where = slice(i * part, (i + 1) * part)
            slope_rest = jnp.dot(
                residual_t[where, half_rows:], active[window:].reshape(half_rows, feats),
                preferred_element_type=F32,
            )
            gradient = slope[where] + 2.0 / total_rows * slope_rest
            moment_one = beta_one * first[where].astype(F32) + (1.0 - beta_one) * gradient
            moment_two = beta_two * second[where].astype(F32) + (1.0 - beta_two) * gradient * gradient
            step[where] = (
                moment_one * (1.0 / bias_one) / (jnp.sqrt(moment_two * (1.0 / bias_two)) + adam_eps)
            ).astype(BF16)
            store(i).start()

        finish_core_last()
        for i in range(4):
            store(i).wait()

    scratch = [
        pltpu.VMEM((feats,), F32),
        pltpu.VMEM((width,), F32),
        pltpu.VMEM((local_rows, width), BF16),
        *(pltpu.VMEM((width, feats), BF16) for _ in range(5)),
        pltpu.SemaphoreType.DMA((7,)),
        pltpu.SemaphoreType.DMA((5,)),
        pltpu.VMEM((local_rows, width), BF16),
        pltpu.VMEM((local_rows, width), BF16),
        pltpu.VMEM((chip_rows, width), F32),
        pltpu.VMEM((2, window, per_chip, chip_rows, width), BF16),
        pltpu.VMEM((chip_rows, width), BF16),
        pltpu.VMEM((peers, 2, core_rows, feats), F32),
        *(pltpu.VMEM((peers, 2, core_rows, feats), BF16) for _ in range(3)),
        pltpu.VMEM((8, feats), F32),
        pltpu.VMEM((peers, 8, feats), F32),
        pltpu.VMEM((2, 2, window, core_rows, width), F32),
        pltpu.VMEM((2, window, core_rows, width), F32),
        pltpu.VMEM((2, window, per_core, chip_rows, width), BF16),
        pltpu.VMEM((2 * window, per_core, chip_rows, width), BF16),
        pltpu.VMEM((per_core, chip_rows, width), F32),
        pltpu.VMEM((per_core, chip_rows, width), BF16),
        pltpu.VMEM((per_core, chip_rows, width), BF16),
        pltpu.VMEM((chip_rows, width), F32),
        pltpu.VMEM((chip_rows, width), F32),
        pltpu.VMEM((2, window, per_chip, chip_rows, width), BF16),
        pltpu.VMEM((chip_rows, width), BF16),
        pltpu.VMEM((1, feats), F32),
        pltpu.VMEM((width, total_rows), BF16),
        pltpu.VMEM((width, feats), F32),
        *(pltpu.SemaphoreType.DMA((4,)) for _ in range(2)),
        *(pltpu.SemaphoreType.DMA((per_chip,)) for _ in range(6)),
        *(pltpu.SemaphoreType.DMA((2 * window * per_chip,)) for _ in range(4)),
        *(pltpu.SemaphoreType.DMA((2 * window,)) for _ in range(4)),
        *(pltpu.SemaphoreType.DMA((2 * window * per_core,)) for _ in range(2)),
        *(pltpu.SemaphoreType.DMA((2 * peers,)) for _ in range(2)),
        *(pltpu.SemaphoreType.DMA((peers,)) for _ in range(2)),
        *(pltpu.SemaphoreType.DMA((2 * peers,)) for _ in range(2)),
    ]
    return kernel, scratch


def hand_over(recon, step):
    parts = 4
    part = step.shape[0] // parts

    def kernel(recon_in, step_in, recon_out, step_out, recon_held, step_held, in_sems, out_sems):
        where = [pl.ds(i * part, part) for i in range(parts)]
        arrive = [pltpu.make_async_copy(recon_in, recon_held, in_sems.at[parts])]
        leave = [pltpu.make_async_copy(recon_held, recon_out, out_sems.at[parts])]
        for i, rows in enumerate(where):
            arrive.append(pltpu.make_async_copy(step_in.at[rows], step_held.at[rows], in_sems.at[i]))
            leave.append(pltpu.make_async_copy(step_held.at[rows], step_out.at[rows], out_sems.at[i]))
        for copy in arrive:
            copy.start()
        for one, two in zip(arrive, leave):
            one.wait()
            two.start()
        for copy in leave:
            copy.wait()

    hbm = pl.BlockSpec(memory_space=pl.ANY)
    return pl.pallas_call(
        kernel,
        out_shape=(
            jax.ShapeDtypeStruct(recon.shape, recon.dtype),
            jax.ShapeDtypeStruct(step.shape, step.dtype),
        ),
        in_specs=[hbm, hbm],
        out_specs=(hbm, hbm),
        scratch_shapes=[
            pltpu.VMEM(recon.shape, recon.dtype),
            pltpu.VMEM(step.shape, step.dtype),
            pltpu.SemaphoreType.DMA((parts + 1,)),
            pltpu.SemaphoreType.DMA((parts + 1,)),
        ],
        compiler_params=pltpu.CompilerParams(vmem_limit_bytes=60 * 2**20),
    )(recon, step)


def shards(nz, rows, reps, activations, enc_weight, enc_bias, dec_weight, dec_bias, first_moment, second_moment):
    local_rows, width = activations.shape
    feats = enc_weight.shape[1]
    kernel, scratch = make_kernel(nz, rows, reps, local_rows, width, feats)
    hbm = pl.BlockSpec(memory_space=pl.ANY)
    recon, step = pl.pallas_call(
        kernel,
        out_shape=(
            jax.ShapeDtypeStruct((local_rows, width), BF16),
            jax.ShapeDtypeStruct((width, feats), BF16),
        ),
        in_specs=[hbm] * 7,
        out_specs=(hbm, hbm),
        scratch_shapes=scratch,
        compiler_params=pltpu.CompilerParams(
            collective_id=0, has_side_effects=True, vmem_limit_bytes=60 * 2**20
        ),
    )(activations, enc_weight, enc_bias, dec_weight.T, dec_bias, first_moment.T, second_moment.T)
    recon, step = hand_over(recon, step)
    return recon, step.T


def solution(mesh):
    nz, rows, reps = mesh.shape["feat"] // 4, mesh.shape["row"], mesh.shape["rep"]

    def step(*args):
        return shards(nz, rows, reps, *args)

    return jax.shard_map(
        step,
        mesh=mesh,
        in_specs=(
            P("feat", ("row", "rep")),
            P(("row", "rep"), "feat"),
            P("feat"),
            P("feat", ("row", "rep")),
            P(("row", "rep")),
            P("feat", ("row", "rep")),
            P("feat", ("row", "rep")),
        ),
        out_specs=(P("feat", ("row", "rep")), P("feat", ("row", "rep"))),
        check_vma=False,
    )
```

```python
import jax
import jax.numpy as jnp
from jax import lax
from jax.experimental import pallas as pl
from jax.experimental.pallas import tpu as pltpu
from jax.sharding import PartitionSpec as P

sparsity_coef = 5.0
beta_one = 0.9
beta_two = 0.999
bias_one = 0.99997344
bias_two = 0.095207853
adam_eps = 1e-08
norm_eps = 1e-06

MESH = pl.DeviceIdType.MESH
F32 = jnp.float32
BF16 = jnp.bfloat16


def make_kernel(nz, rows, reps, local_rows, width, feats):
    near = (0, 1, 2, -1)
    window = len(near)
    per_chip = nz // window
    per_core = per_chip // 2
    chip_rows = 2 * local_rows
    total_rows = 2 * nz * chip_rows
    half_rows = total_rows // 2
    peers = rows * reps
    group = total_rows // peers
    core_rows = per_core * chip_rows
    assert peers == 2 * window and group == 2 * core_rows
    around = [(far, w) for far in (1, 0) for w in range(window) if (far, w) != (0, 0)]

    def kernel(
        act_hbm, enc_hbm, ebias_hbm, dec_hbm, dbias_hbm, first_hbm, second_hbm,
        recon_hbm, step_hbm,
        ebias_ref, dbias_ref, recon_ref, enc, dec, first, second, step, load_sem, store_sem,
        act_send, act_recv, acts, gathered, block, partial, sums_out, sums_in, active,
        squares_out, squares_in, product, core_in, parts_out, parts_in, own_part, z_out, z_in, total_out, total_in, residuals,
        block_two, coef, residual_t, slope,
        pair_send, pair_recv, z_send, z_recv, zr_send, zr_recv, za_send, za_recv,
        x_send, x_recv, xa_send, xa_recv, c_send, c_recv, ca_send, ca_recv, part_send, part_recv,
        peer_send, peer_recv, sq_send, sq_recv, ac_send, ac_recv,
    ):
        feat = lax.axis_index("feat")
        row, rep = lax.axis_index("row"), lax.axis_index("rep")
        far_x = lax.div(feat, 2 * nz)
        z = lax.rem(lax.div(feat, 2), nz)
        core = lax.rem(feat, 2)
        k = row * reps + rep

        def chip(far, where):
            x = lax.rem(far_x + far, 2)
            return (x * (2 * nz) + lax.rem(where + 2 * nz, nz) * 2 + core, row, rep)

        other_core = (feat + 1 - 2 * core, row, rep)

        def peer(j):
            p = lax.rem(k + j, peers)
            return (feat, lax.div(p, reps), lax.rem(p, reps))

        loads = [
            pltpu.make_async_copy(src, dst, load_sem.at[i])
            for i, (src, dst) in enumerate(
                (
                    (act_hbm, act_send), (dbias_hbm, dbias_ref), (dec_hbm, dec), (enc_hbm, enc),
                    (ebias_hbm, ebias_ref), (first_hbm, first), (second_hbm, second),
                )
            )
        ]
        barrier = pltpu.get_barrier_semaphore()

        def greet(device):
            pl.semaphore_signal(barrier, inc=1, device_id=device, device_id_type=MESH)

        def far_first(j):
            return jnp.where(core == 0, j, per_chip - 1 - j)

        def away(m):
            return window * (m - per_core) + window // 2

        @pl.loop(0, per_core)
        def _(j):
            greet(chip(0, z + away(far_first(j))))
            greet(chip(0, z - away(far_first(j))))

        beside = sorted({(far, side * near[w]) for far, w in around for side in (1, -1)})
        for far, offset in beside:
            greet(chip(far, z + offset))
        greet(other_core)

        @pl.loop(1, peers)
        def _(j):
            greet(peer(j))

        for load in loads:
            load.start()
        for load in loads[:3]:
            load.wait()
        wide = dec[...].astype(F32)
        square = wide * wide
        high = square.astype(BF16)
        rest = (square - high.astype(F32)).astype(BF16)
        ones = jnp.ones((8, width), BF16)
        squares_out[...] = jnp.dot(ones, high, preferred_element_type=F32) + jnp.dot(
            ones, rest, preferred_element_type=F32
        )
        pl.semaphore_wait(barrier, 2 * per_core + len(beside) + peers)

        def pair(src, dst, i, device):
            return pltpu.make_async_remote_copy(
                src_ref=src, dst_ref=dst, send_sem=pair_send.at[i], recv_sem=pair_recv.at[i],
                device_id=device, device_id_type=MESH,
            )

        def square_copy(j):
            return pltpu.make_async_remote_copy(
                src_ref=squares_out, dst_ref=squares_in.at[j], send_sem=sq_send.at[j], recv_sem=sq_recv.at[j],
                device_id=peer(j), device_id_type=MESH,
            )

        swap = pair(act_send, act_recv, 0, other_core)
        swap.start()
        swap.wait()
        own, his = act_send[...].astype(F32), act_recv[...].astype(F32)
        acts[0:local_rows] = jnp.where(core == 0, own, his)
        acts[local_rows:] = jnp.where(core == 0, his, own)
        block[...] = (acts[...] - dbias_ref[...].reshape(1, width)).astype(BF16)

        def each_far(action):
            @pl.loop(0, per_core)
            def _(j):
                action(far_first(j))

        def each_mine(action):
            @pl.loop(0, per_core)
            def _(i):
                action(core * per_core + i)

        mine = pl.ds(core * per_core, per_core)

        def gather(src, buffer, z_sems, x_sems, core_sems, between):
            def z_copy(m):
                return pltpu.make_async_remote_copy(
                    src_ref=src, dst_ref=buffer.at[0, 0, m], send_sem=z_sems[0].at[m], recv_sem=z_sems[1].at[m],
                    device_id=chip(0, z - away(m)), device_id_type=MESH,
                )

            def beside_copy(far, w, m):
                i = (far * window + w) * per_chip + m
                return pltpu.make_async_remote_copy(
                    src_ref=buffer.at[0, 0, m], dst_ref=buffer.at[far, w, m],
                    send_sem=x_sems[0].at[i], recv_sem=x_sems[1].at[i],
                    device_id=chip(far, z + near[w]), device_id_type=MESH,
                )

            def core_copy(far, w):
                return pltpu.make_async_remote_copy(
                    src_ref=buffer.at[far, w, mine], dst_ref=buffer.at[far, w, mine],
                    send_sem=core_sems[0].at[far * window + w], recv_sem=core_sems[1].at[far * window + w],
                    device_id=other_core, device_id_type=MESH,
                )

            each_far(lambda m: z_copy(m).start())

            between()

            @pl.loop(0, per_core)
            def _(i):
                m = far_first(per_core - 1 - i)
                z_copy(m).wait_recv()
                for far, w in around:
                    beside_copy(far, w, m).start()

            core_copy(0, 0).start()

            def arrive(far):
                for w in range(window):
                    if (far, w) != (0, 0):
                        each_mine(lambda m: beside_copy(far, w, m).wait_recv())
                        core_copy(far, w).start()
                for w in range(window):
                    core_copy(far, w).wait_recv()

            def finish_beside():
                each_far(lambda m: z_copy(m).wait_send())
                for far, w in around:
                    each_mine(lambda m: beside_copy(far, w, m).wait_send())

            def finish_core():
                for i in range(2 * window):
                    core_copy(i // window, i % window).wait_send()

            return arrive, finish_beside, finish_core

        def during_first():
            @pl.loop(1, peers)
            def _(j):
                square_copy(j).start()

            loads[3].wait()
            loads[4].wait()

        arrive, finish_beside, finish_core = gather(
            block, gathered, (z_send, z_recv), (x_send, x_recv), (c_send, c_recv), during_first
        )

        def sum_copy(j, who):
            p = lax.rem(k + j, peers)
            return p, pltpu.make_async_remote_copy(
                src_ref=sums_out.at[p, who], dst_ref=sums_in.at[j, who],
                send_sem=peer_send.at[2 * j + who], recv_sem=peer_recv.at[2 * j + who],
                device_id=peer(j), device_id_type=MESH,
            )

        halves = (1 - core, core)

        def encode(far):
            rows_in = gathered[far].reshape(half_rows, width)
            value = jnp.dot(rows_in, enc[...], preferred_element_type=F32).reshape(window, 2, core_rows, feats)
            partial[far * window : (far + 1) * window] = value
            sums_out[far * window : (far + 1) * window] = value.astype(BF16)
            for who in halves:

                @pl.loop(1, peers)
                def _(j):
                    p, copy = sum_copy(j, who)

                    @pl.when(lax.div(p, window) == far)
                    def _():
                        copy.start()

        arrive(0)
        encode(0)
        arrive(1)
        encode(1)

        def active_copy(j, who):
            return pltpu.make_async_remote_copy(
                src_ref=active.at[k, who], dst_ref=active.at[k, who],
                send_sem=ac_send.at[2 * j + who], recv_sem=ac_recv.at[2 * j + who],
                device_id=peer(j), device_id_type=MESH,
            )

        for who in halves:
            pre_sum = partial[k, who] + ebias_ref[...].reshape(1, feats)
            for j in range(1, peers):
                sum_copy(j, who)[1].wait_recv()
                pre_sum += sums_in[j, who].astype(F32)
            active[k, who] = jnp.maximum(pre_sum, 0.0).astype(BF16)

            @pl.loop(1, peers)
            def _(j):
                active_copy(j, who).start()

        def wait_active(far, who):
            @pl.loop(1, peers)
            def _(j):
                @pl.when(lax.div(lax.rem(k - j + peers, peers), window) == far)
                def _():
                    active_copy(j, who).wait_recv()

        def decode(far, who):
            value = lax.dot_general(
                active[far * window : (far + 1) * window, who].reshape(window * core_rows, feats),
                dec[...], (((1,), (1,)), ((), ())), preferred_element_type=F32,
            )
            product[far, who] = value.reshape(window, core_rows, width)

        core_parts = [pair(product.at[far, 1 - core], core_in.at[far], 1 + far, other_core) for far in (0, 1)]

        def part_copy(far, w, place):
            i = (far * window + w) * per_core + place
            return pltpu.make_async_remote_copy(
                src_ref=parts_out.at[far, w, place], dst_ref=parts_in.at[far * window + w, place],
                send_sem=part_send.at[i], recv_sem=part_recv.at[i],
                device_id=chip(far, z - near[w]), device_id_type=MESH,
            )

        def place_of(j):
            return jnp.where(core == 0, j, per_core - 1 - j)

        def hand_out(far):
            core_parts[far].wait_recv()
            both_cores = product[far, core] + core_in[far]
            both_cores = both_cores.reshape(window, per_core, chip_rows, width)
            parts_out[far] = both_cores.astype(BF16)

            @pl.loop(0, per_core)
            def _(j):
                for other, w in around:
                    if other == far:
                        part_copy(far, w, place_of(j)).start()

            return both_cores

        wait_active(0, 1 - core)
        decode(0, 1 - core)
        core_parts[0].start()
        wait_active(1, 1 - core)
        decode(1, 1 - core)
        core_parts[1].start()
        wait_active(0, core)
        decode(0, core)
        own_part[...] = hand_out(0)[0]
        wait_active(1, core)
        decode(1, core)
        hand_out(1)

        def back_copy(m):
            place = m - core * per_core
            return pltpu.make_async_remote_copy(
                src_ref=z_out.at[place], dst_ref=z_in.at[place], send_sem=zr_send.at[m], recv_sem=zr_recv.at[m],
                device_id=chip(0, z + away(m)), device_id_type=MESH,
            )

        @pl.loop(0, per_core)
        def _(j):
            place = place_of(j)
            value = own_part[place]
            for far, w in reversed(around):
                part_copy(far, w, place).wait_recv()
                value += parts_in[far * window + w, place].astype(F32)
            z_out[place] = value.astype(BF16)
            back_copy(far_first(j)).start()

        flat = active[...].reshape(total_rows, feats)
        counts = jnp.dot(jnp.ones((8, total_rows), BF16), flat, preferred_element_type=F32)
        sum_squares = squares_out[...]
        for j in range(1, peers):
            square_copy(j).wait_recv()
            sum_squares += squares_in[j]
        norm = jnp.sqrt(sum_squares[0:1] + norm_eps)
        coef[...] = sparsity_coef / total_rows * counts[0:1] / norm

        each_far(lambda m: back_copy(m).wait_recv())
        total_out[...] = jnp.sum(z_in[...].astype(F32), axis=0)
        both = pair(total_out, total_in, 3, other_core)
        both.start()
        both.wait_recv()
        rebuilt = total_out[...] + total_in[...] + dbias_ref[...].reshape(1, width)
        recon_ref[...] = jnp.where(core == 0, rebuilt[0:local_rows], rebuilt[local_rows:]).astype(BF16)
        store_recon = pltpu.make_async_copy(recon_ref, recon_hbm, store_sem.at[4])
        store_recon.start()
        block_two[...] = (rebuilt - acts[...]).astype(BF16)

        def during_last():
            loads[5].wait()
            loads[6].wait()
            store_recon.wait()
            finish_beside()
            finish_core()
            each_far(lambda m: back_copy(m).wait_send())
            for copy in (*core_parts, both):
                copy.wait_send()

            @pl.loop(0, per_core)
            def _(j):
                for far, w in around:
                    part_copy(far, w, j).wait_send()

            @pl.loop(1, peers)
            def _(j):
                square_copy(j).wait_send()
                for who in (0, 1):
                    sum_copy(j, who)[1].wait_send()
                    active_copy(j, who).wait_send()


        arrive, finish_beside_last, finish_core_last = gather(
            block_two, residuals, (za_send, za_recv), (xa_send, xa_recv), (ca_send, ca_recv), during_last
        )

        def turn(far):
            residual_t[:, far * half_rows : (far + 1) * half_rows] = residuals[far].reshape(half_rows, width).T

        arrive(0)
        turn(0)
        slope[...] = 2.0 / total_rows * jnp.dot(
            residual_t[:, :half_rows], active[:window].reshape(half_rows, feats), preferred_element_type=F32
        ) + coef[...] * dec[...].astype(F32)
        finish_beside_last()
        arrive(1)
        turn(1)

        part = width // 4

        def store(i):
            where = pl.ds(i * part, part)
            return pltpu.make_async_copy(step.at[where], step_hbm.at[where], store_sem.at[i])

        for i in range(4):
            where = slice(i * part, (i + 1) * part)
            slope_rest = jnp.dot(
                residual_t[where, half_rows:], active[window:].reshape(half_rows, feats),
                preferred_element_type=F32,
            )
            gradient = slope[where] + 2.0 / total_rows * slope_rest
            moment_one = beta_one * first[where].astype(F32) + (1.0 - beta_one) * gradient
            moment_two = beta_two * second[where].astype(F32) + (1.0 - beta_two) * gradient * gradient
            step[where] = (
                moment_one * (1.0 / bias_one) / (jnp.sqrt(moment_two * (1.0 / bias_two)) + adam_eps)
            ).astype(BF16)
            store(i).start()

        finish_core_last()
        for i in range(4):
            store(i).wait()

    scratch = [
        pltpu.VMEM((feats,), F32),
        pltpu.VMEM((width,), F32),
        pltpu.VMEM((local_rows, width), BF16),
        *(pltpu.VMEM((width, feats), BF16) for _ in range(5)),
        pltpu.SemaphoreType.DMA((7,)),
        pltpu.SemaphoreType.DMA((5,)),
        pltpu.VMEM((local_rows, width), BF16),
        pltpu.VMEM((local_rows, width), BF16),
        pltpu.VMEM((chip_rows, width), F32),
        pltpu.VMEM((2, window, per_chip, chip_rows, width), BF16),
        pltpu.VMEM((chip_rows, width), BF16),
        pltpu.VMEM((peers, 2, core_rows, feats), F32),
        *(pltpu.VMEM((peers, 2, core_rows, feats), BF16) for _ in range(3)),
        pltpu.VMEM((8, feats), F32),
        pltpu.VMEM((peers, 8, feats), F32),
        pltpu.VMEM((2, 2, window, core_rows, width), F32),
        pltpu.VMEM((2, window, core_rows, width), F32),
        pltpu.VMEM((2, window, per_core, chip_rows, width), BF16),
        pltpu.VMEM((2 * window, per_core, chip_rows, width), BF16),
        pltpu.VMEM((per_core, chip_rows, width), F32),
        pltpu.VMEM((per_core, chip_rows, width), BF16),
        pltpu.VMEM((per_core, chip_rows, width), BF16),
        pltpu.VMEM((chip_rows, width), F32),
        pltpu.VMEM((chip_rows, width), F32),
        pltpu.VMEM((2, window, per_chip, chip_rows, width), BF16),
        pltpu.VMEM((chip_rows, width), BF16),
        pltpu.VMEM((1, feats), F32),
        pltpu.VMEM((width, total_rows), BF16),
        pltpu.VMEM((width, feats), F32),
        *(pltpu.SemaphoreType.DMA((4,)) for _ in range(2)),
        *(pltpu.SemaphoreType.DMA((per_chip,)) for _ in range(6)),
        *(pltpu.SemaphoreType.DMA((2 * window * per_chip,)) for _ in range(4)),
        *(pltpu.SemaphoreType.DMA((2 * window,)) for _ in range(4)),
        *(pltpu.SemaphoreType.DMA((2 * window * per_core,)) for _ in range(2)),
        *(pltpu.SemaphoreType.DMA((2 * peers,)) for _ in range(2)),
        *(pltpu.SemaphoreType.DMA((peers,)) for _ in range(2)),
        *(pltpu.SemaphoreType.DMA((2 * peers,)) for _ in range(2)),
    ]
    return kernel, scratch


def hand_over(recon, step):
    parts = 4
    part = step.shape[0] // parts

    def kernel(recon_in, step_in, recon_out, step_out, recon_held, step_held, in_sems, out_sems):
        where = [pl.ds(i * part, part) for i in range(parts)]
        arrive = [pltpu.make_async_copy(recon_in, recon_held, in_sems.at[parts])]
        leave = [pltpu.make_async_copy(recon_held, recon_out, out_sems.at[parts])]
        for i, rows in enumerate(where):
            arrive.append(pltpu.make_async_copy(step_in.at[rows], step_held.at[rows], in_sems.at[i]))
            leave.append(pltpu.make_async_copy(step_held.at[rows], step_out.at[rows], out_sems.at[i]))
        for copy in arrive:
            copy.start()
        for one, two in zip(arrive, leave):
            one.wait()
            two.start()
        for copy in leave:
            copy.wait()

    hbm = pl.BlockSpec(memory_space=pl.ANY)
    return pl.pallas_call(
        kernel,
        out_shape=(
            jax.ShapeDtypeStruct(recon.shape, recon.dtype),
            jax.ShapeDtypeStruct(step.shape, step.dtype),
        ),
        in_specs=[hbm, hbm],
        out_specs=(hbm, hbm),
        scratch_shapes=[
            pltpu.VMEM(recon.shape, recon.dtype),
            pltpu.VMEM(step.shape, step.dtype),
            pltpu.SemaphoreType.DMA((parts + 1,)),
            pltpu.SemaphoreType.DMA((parts + 1,)),
        ],
        compiler_params=pltpu.CompilerParams(vmem_limit_bytes=60 * 2**20),
    )(recon, step)


def shards(nz, rows, reps, activations, enc_weight, enc_bias, dec_weight, dec_bias, first_moment, second_moment):
    local_rows, width = activations.shape
    feats = enc_weight.shape[1]
    kernel, scratch = make_kernel(nz, rows, reps, local_rows, width, feats)
    hbm = pl.BlockSpec(memory_space=pl.ANY)
    recon, step = pl.pallas_call(
        kernel,
        out_shape=(
            jax.ShapeDtypeStruct((local_rows, width), BF16),
            jax.ShapeDtypeStruct((width, feats), BF16),
        ),
        in_specs=[hbm] * 7,
        out_specs=(hbm, hbm),
        scratch_shapes=scratch,
        compiler_params=pltpu.CompilerParams(
            collective_id=0, has_side_effects=True, vmem_limit_bytes=60 * 2**20
        ),
    )(activations, enc_weight, enc_bias, dec_weight.T, dec_bias, first_moment.T, second_moment.T)
    recon, step = hand_over(recon, step)
    return recon, step.T


def solution(mesh):
    nz, rows, reps = mesh.shape["feat"] // 4, mesh.shape["row"], mesh.shape["rep"]

    def step(*args):
        return shards(nz, rows, reps, *args)

    return jax.shard_map(
        step,
        mesh=mesh,
        in_specs=(
            P("feat", ("row", "rep")),
            P(("row", "rep"), "feat"),
            P("feat"),
            P("feat", ("row", "rep")),
            P(("row", "rep")),
            P("feat", ("row", "rep")),
            P("feat", ("row", "rep")),
        ),
        out_specs=(P("feat", ("row", "rep")), P("feat", ("row", "rep"))),
        check_vma=False,
    )
```
